32 devices in a mesh: dp: 16 (over z, y, x), tensor: 2 (over core).
Axes of the slice: x: 2, y: 2, z: 4, core: 2. Of those that a mesh axis runs over, the one named last changes fastest.
Arguments:
- inputs: bfloat16 [16384, 1024], P(('dp', 'tensor')), may hold values from -6 to 6
- cotangent: bfloat16 [16384, 1024], P(('dp', 'tensor')), may hold values from -6 to 6
- slot_flags: int32 [16], P('dp'), may hold values 0 or 1
- early_norm_gain: float32 [1024], replicated, may hold values from 0.1 to 1.9
- early_norm_shift: float32 [1024], replicated, may hold values from -3 to 3
- early_up: bfloat16 [1024, 4096], P(None, 'tensor'), may hold values from -0.1875 to 0.1875
- early_up_bias: float32 [4096], P('tensor'), may hold values from -3 to 3
- early_down: bfloat16 [4096, 1024], P('tensor'), may hold values from -0.1875 to 0.1875
- early_down_bias: float32 [1024], replicated, may hold values from -3 to 3
- attend_norm_gain: float32 [1024], replicated, may hold values from 0.1 to 1.9
- attend_norm_shift: float32 [1024], replicated, may hold values from -3 to 3
- query_weight: bfloat16 [1024, 1024], P(None, 'tensor'), may hold values from -0.1875 to 0.1875
- query_bias: float32 [1024], P('tensor'), may hold values from -3 to 3
- key_weight: bfloat16 [1024, 1024], P(None, 'tensor'), may hold values from -0.1875 to 0.1875
- value_weight: bfloat16 [1024, 1024], P(None, 'tensor'), may hold values from -0.1875 to 0.1875
- value_bias: float32 [1024], P('tensor'), may hold values from -3 to 3
- distance_table: float32 [73, 64], replicated, may hold values from -6 to 6
- attend_weight: bfloat16 [1024, 1024], P('tensor'), may hold values from -1 to 1
- attend_bias: float32 [1024], replicated, may hold values from -3 to 3
- mixer_norm_gain: float32 [1024], replicated, may hold values from 0.1 to 1.9
- mixer_norm_shift: float32 [1024], replicated, may hold values from -3 to 3
- gated_weight: bfloat16 [2, 1024, 1024], P(None, None, 'tensor'), may hold values from -0.1875 to 0.1875
- depth_kernel: float32 [31, 1024], P(None, 'tensor'), may hold values from -1 to 1
- depth_norm_gain: float32 [1024], P('tensor'), may hold values from 0.1 to 1.9
- depth_norm_shift: float32 [1024], P('tensor'), may hold values from -3 to 3
- mixer_out: bfloat16 [1024, 1024], P('tensor'), may hold values from -0.25 to 0.25
- late_norm_gain: float32 [1024], replicated, may hold values from 0.1 to 1.9
- late_norm_shift: float32 [1024], replicated, may hold values from -3 to 3
- late_up: bfloat16 [1024, 4096], P(None, 'tensor'), may hold values from -0.1875 to 0.1875
- late_up_bias: float32 [4096], P('tensor'), may hold values from -3 to 3
- late_down: bfloat16 [4096, 1024], P('tensor'), may hold values from -0.1875 to 0.1875
- late_down_bias: float32 [1024], replicated, may hold values from -3 to 3
- final_gain: float32 [1024], replicated, may hold values from 0.1 to 1.9
- final_shift: float32 [1024], replicated, may hold values from -3 to 3
Outputs:
- output: bfloat16 [16384, 1024], P(('dp', 'tensor'))
- input_gradient: float32 [16384, 1024], P(('dp', 'tensor'))
- early_norm_gain_gradient: float32 [1024], replicated
- early_norm_shift_gradient: float32 [1024], replicated
- early_up_gradient: float32 [1024, 4096], P('dp', 'tensor')
- early_up_bias_gradient: float32 [4096], P('tensor')
- early_down_gradient: float32 [4096, 1024], P('tensor', 'dp')
- early_down_bias_gradient: float32 [1024], replicated
- attend_norm_gain_gradient: float32 [1024], replicated
- attend_norm_shift_gradient: float32 [1024], replicated
- query_weight_gradient: float32 [1024, 1024], P('dp', 'tensor')
- query_bias_gradient: float32 [1024], P('tensor')
- key_weight_gradient: float32 [1024, 1024], P('dp', 'tensor')
- value_weight_gradient: float32 [1024, 1024], P('dp', 'tensor')
- value_bias_gradient: float32 [1024], P('tensor')
- distance_table_gradient: float32 [73, 64], replicated
- attend_weight_gradient: float32 [1024, 1024], P('tensor', 'dp')
- attend_bias_gradient: float32 [1024], replicated
- mixer_norm_gain_gradient: float32 [1024], replicated
- mixer_norm_shift_gradient: float32 [1024], replicated
- gated_weight_gradient: float32 [2, 1024, 1024], P(None, 'dp', 'tensor')
- depth_kernel_gradient: float32 [31, 1024], P(None, 'tensor')
- depth_norm_gain_gradient: float32 [1024], P('tensor')
- depth_norm_shift_gradient: float32 [1024], P('tensor')
- mixer_out_gradient: float32 [1024, 1024], P('tensor', 'dp')
- late_norm_gain_gradient: float32 [1024], replicated
- late_norm_shift_gradient: float32 [1024], replicated
- late_up_gradient: float32 [1024, 4096], P('dp', 'tensor')
- late_up_bias_gradient: float32 [4096], P('tensor')
- late_down_gradient: float32 [4096, 1024], P('tensor', 'dp')
- late_down_bias_gradient: float32 [1024], replicated
- final_gain_gradient: float32 [1024], replicated
- final_shift_gradient: float32 [1024], replicated
The draws below stay inside these ranges and needn't reach their ends.
Inputs may be any that keep to these rules, and one draw needn't show every extreme that they name: `slot_flags`: 1 where the slot holds a clip, 0 where it is empty.
All inputs are finite; a program needn't handle non-finite values. No bound on the sum of `slot_flags` on one device may be relied on, other than what follows from the above.
Results may differ from the reference program's by a relative error of at most 0.03.
Values may be sent and summed in bfloat16 or wider, within the bound.
No kernel may reach another device: no remote copies, remote signals or barrier semaphores. Data moves between devices by JAX's collectives and lax.ppermute only.
A program may use at most 256 MiB of HBM per device.

```python
import jax
import jax.numpy as jnp
from jax import lax

D = 1024
HEADS = 16
HEAD_DIM = 64
FF = 4096
KERNEL = 31
LEFT = 64
RIGHT = 8
LEN = 1024
REL = 73
BLOCK = 512
TOKENS = 16384
N_DP = 16


def set_ends(drawn, own_key, least, largest):
    longest = drawn.shape.index(max(drawn.shape))
    spots = []
    for shift in (0, 1):
        where = [jax.random.randint(jax.random.fold_in(own_key, axis), (), 0, length) for axis, length in enumerate(drawn.shape)]
        where[longest] = (where[longest] + shift) % drawn.shape[longest]
        spots.append(tuple(where))
    return drawn.at[spots[0]].set(least).at[spots[1]].set(largest)


def shard_levels(key, dims, split, low, high):
    loudness, own = 1.0, jax.random.fold_in(key, 6)
    for dim, parts in split:
        heights = jnp.exp(jax.random.uniform(jax.random.fold_in(own, dim), (parts,), jnp.float32, low / len(split), high / len(split)))
        loudness = loudness * jnp.repeat(heights, dims[dim] // parts).reshape([-1 if axis == dim else 1 for axis in range(len(dims))])
    return loudness


def centred(own_key, dims, scale, bound, split=(), kind=jnp.bfloat16):
    level = shard_levels(own_key, dims, split, -0.22, 0.18) if split else 1.0
    values = jax.random.normal(own_key, dims, jnp.float32) * scale * level
    return jnp.minimum(jnp.maximum(values, -bound), bound).astype(kind)


def setup_inputs(seed: int = 0) -> dict:
    key_of = jax.random.split(jax.random.key(seed), 35)
    inputs = centred(key_of[0], (TOKENS, D), 1.0, 6.0, ((0, 32),))
    cotangent = centred(key_of[1], (TOKENS, D), 1.0, 6.0, ((0, 32),))
    slot_flags = set_ends((jax.random.randint(key_of[2], (N_DP,), 0, 4) < 3).astype(jnp.int32), jax.random.fold_in(key_of[2], 1), 0, 1)
    early_norm_gain = jnp.clip(1.0 + 0.18 * jax.random.normal(key_of[3], (D,), jnp.float32), 0.1, 1.9)
    early_norm_shift = centred(key_of[4], (D,), 0.5, 3.0, (), jnp.float32)
    early_up = centred(key_of[5], (D, FF), D ** -0.5, 0.1875, ((1, 2),))
    early_up_bias = centred(key_of[6], (FF,), 0.5, 3.0, ((0, 2),), jnp.float32)
    early_down = centred(key_of[7], (FF, D), (FF // 4) ** -0.5, 0.1875, ((0, 2),))
    early_down_bias = centred(key_of[8], (D,), 0.5, 3.0, (), jnp.float32)
    attend_norm_gain = jnp.clip(1.0 + 0.18 * jax.random.normal(key_of[9], (D,), jnp.float32), 0.1, 1.9)
    attend_norm_shift = centred(key_of[10], (D,), 0.5, 3.0, (), jnp.float32)
    query_weight = centred(key_of[11], (D, D), D ** -0.5, 0.1875, ((1, 2),))
    query_bias = centred(key_of[12], (D,), 0.5, 3.0, ((0, 2),), jnp.float32)
    key_weight = centred(key_of[13], (D, D), D ** -0.5, 0.1875, ((1, 2),))
    value_weight = centred(key_of[14], (D, D), D ** -0.5, 0.1875, ((1, 2),))
    value_bias = centred(key_of[15], (D,), 0.5, 3.0, ((0, 2),), jnp.float32)
    distance_table = centred(key_of[16], (REL, HEAD_DIM), 1.0, 6.0, (), jnp.float32)
    attend_weight = centred(key_of[17], (D, D), (D // 32) ** -0.5, 1.0, ((0, 2),))
    attend_bias = centred(key_of[18], (D,), 0.5, 3.0, (), jnp.float32)
    mixer_norm_gain = jnp.clip(1.0 + 0.18 * jax.random.normal(key_of[19], (D,), jnp.float32), 0.1, 1.9)
    mixer_norm_shift = centred(key_of[20], (D,), 0.5, 3.0, (), jnp.float32)
    gated_weight = centred(key_of[21], (2, D, D), D ** -0.5, 0.1875, ((2, 2),))
    depth_kernel = centred(key_of[22], (KERNEL, D), KERNEL ** -0.5, 1.0, ((1, 2),), jnp.float32)
    depth_norm_gain = jnp.clip(1.0 + 0.18 * jax.random.normal(key_of[23], (D,), jnp.float32), 0.1, 1.9)
    depth_norm_shift = centred(key_of[24], (D,), 0.5, 3.0, ((0, 2),), jnp.float32)
    mixer_out = centred(key_of[25], (D, D), (D // 2) ** -0.5, 0.25, ((0, 2),))
    late_norm_gain = jnp.clip(1.0 + 0.18 * jax.random.normal(key_of[26], (D,), jnp.float32), 0.1, 1.9)
    late_norm_shift = centred(key_of[27], (D,), 0.5, 3.0, (), jnp.float32)
    late_up = centred(key_of[28], (D, FF), D ** -0.5, 0.1875, ((1, 2),))
    late_up_bias = centred(key_of[29], (FF,), 0.5, 3.0, ((0, 2),), jnp.float32)
    late_down = centred(key_of[30], (FF, D), (FF // 4) ** -0.5, 0.1875, ((0, 2),))
    late_down_bias = centred(key_of[31], (D,), 0.5, 3.0, (), jnp.float32)
    final_gain = jnp.clip(1.0 + 0.18 * jax.random.normal(key_of[32], (D,), jnp.float32), 0.1, 1.9)
    final_shift = centred(key_of[33], (D,), 0.5, 3.0, (), jnp.float32)
    return {"inputs": inputs, "cotangent": cotangent, "slot_flags": slot_flags, "early_norm_gain": early_norm_gain, "early_norm_shift": early_norm_shift, "early_up": early_up, "early_up_bias": early_up_bias, "early_down": early_down, "early_down_bias": early_down_bias, "attend_norm_gain": attend_norm_gain, "attend_norm_shift": attend_norm_shift, "query_weight": query_weight, "query_bias": query_bias, "key_weight": key_weight, "value_weight": value_weight, "value_bias": value_bias, "distance_table": distance_table, "attend_weight": attend_weight, "attend_bias": attend_bias, "mixer_norm_gain": mixer_norm_gain, "mixer_norm_shift": mixer_norm_shift, "gated_weight": gated_weight, "depth_kernel": depth_kernel, "depth_norm_gain": depth_norm_gain, "depth_norm_shift": depth_norm_shift, "mixer_out": mixer_out, "late_norm_gain": late_norm_gain, "late_norm_shift": late_norm_shift, "late_up": late_up, "late_up_bias": late_up_bias, "late_down": late_down, "late_down_bias": late_down_bias, "final_gain": final_gain, "final_shift": final_shift}


@jax.custom_vjp
def low(v):
    return lax.optimization_barrier(v.astype(jnp.bfloat16)).astype(jnp.float32)

@jax.custom_vjp
def low_back(v):
    return v

def low_keep(v):
    return (low(v), None)

def low_pass(kept, grad):
    return (grad,)

def back_keep(v):
    return (v, None)

def back_low(kept, grad):
    return (low(grad),)
low.defvjp(low_keep, low_pass)
low_back.defvjp(back_keep, back_low)
highest = lax.Precision.HIGHEST
epsilon = 1e-05

def matmul(left, right):
    return jnp.dot(left, right, precision=highest, preferred_element_type=jnp.float32)

def swish(values):
    return values * jax.nn.sigmoid(values)

def layer_norm(values, gain, shift):
    center = values - lax.optimization_barrier(jnp.mean(values, axis=-1, keepdims=True))
    spread = lax.optimization_barrier(jnp.mean(center * center, axis=-1, keepdims=True))
    return center * lax.rsqrt(spread + epsilon) * gain + shift

def relative_index(start, count, length):
    rows = start + lax.broadcasted_iota(jnp.int32, (count, length), 0)
    columns = lax.broadcasted_iota(jnp.int32, (count, length), 1)
    return (jnp.clip(columns - rows, -LEFT, RIGHT) + LEFT).astype(jnp.int32)

def depthwise(signal, kernel):
    taps = kernel.shape[0]
    length = signal.shape[0]
    padded = jnp.pad(signal, ((taps - 1, 0), (0, 0)))
    total = jnp.zeros_like(signal)
    for index in range(taps):
        total = total + kernel[index] * padded[index:index + length]
    return total

def feed_forward(residual, gain, shift, up_weight, up_bias, down_weight, down_bias):
    normed = low(layer_norm(residual, gain, shift))
    hidden = low_back(matmul(normed, up_weight) + up_bias)
    branch = low_back(matmul(low(swish(hidden)), down_weight) + down_bias)
    return residual + 0.5 * branch

def attention(residual, gain, shift, query_weight, query_bias, key_weight, value_weight, value_bias, table, out_weight, out_bias):
    normed = low(layer_norm(residual, gain, shift))
    length = residual.shape[0]

    def heads_of(values):
        return values.reshape(length, HEADS, HEAD_DIM)
    queries = heads_of(low(low_back(matmul(normed, query_weight) + query_bias)))
    keys_all = heads_of(low(low_back(matmul(normed, key_weight))))
    values_all = heads_of(low(low_back(matmul(normed, value_weight) + value_bias)))
    relative = low_back(jnp.einsum('qhd,rd->hqr', queries, table, precision=highest))
    scale = HEAD_DIM ** (-0.5)

    def one_block(start):
        rows = lax.dynamic_slice_in_dim(queries, start, BLOCK, 0)
        table_rows = lax.dynamic_slice_in_dim(relative, start, BLOCK, 1)
        scores = jnp.einsum('qhd,khd->hqk', rows, keys_all, precision=highest)
        where = jnp.broadcast_to(relative_index(start, BLOCK, length)[None], scores.shape)
        scores = low_back((scores + jnp.take_along_axis(table_rows, where, axis=2)) * scale)
        peak = lax.optimization_barrier(jnp.max(scores, axis=2, keepdims=True))
        exponent = jnp.exp(scores - peak)
        probability = low(exponent / lax.optimization_barrier(jnp.sum(exponent, axis=2, keepdims=True)))
        return jnp.einsum('hqk,khd->qhd', probability, values_all, precision=highest)
    starts = jnp.arange(length // BLOCK, dtype=jnp.int32) * BLOCK
    mixed = lax.map(jax.checkpoint(one_block), starts).reshape(length, HEADS * HEAD_DIM)
    mixed = low(low_back(mixed))
    return residual + low_back(matmul(mixed, out_weight) + out_bias)

def mixer(residual, gain, shift, gated_weight, depth_kernel, depth_gain, depth_shift, out_weight):
    normed = low(layer_norm(residual, gain, shift))
    linear = low_back(matmul(normed, gated_weight[0]))
    gates = low_back(matmul(normed, gated_weight[1]))
    glu = linear * jax.nn.sigmoid(gates)
    mixed = layer_norm(depthwise(glu, depth_kernel), depth_gain, depth_shift)
    branch = low_back(matmul(low(swish(mixed)), out_weight))
    return residual + branch

def reference(inputs, cotangent, slot_flags, early_norm_gain, early_norm_shift, early_up, early_up_bias, early_down, early_down_bias, attend_norm_gain, attend_norm_shift, query_weight, query_bias, key_weight, value_weight, value_bias, distance_table, attend_weight, attend_bias, mixer_norm_gain, mixer_norm_shift, gated_weight, depth_kernel, depth_norm_gain, depth_norm_shift, mixer_out, late_norm_gain, late_norm_shift, late_up, late_up_bias, late_down, late_down_bias, final_gain, final_shift):
    listed = (early_norm_gain, early_norm_shift, early_up, early_up_bias, early_down, early_down_bias, attend_norm_gain, attend_norm_shift, query_weight, query_bias, key_weight, value_weight, value_bias, distance_table, attend_weight, attend_bias, mixer_norm_gain, mixer_norm_shift, gated_weight, depth_kernel, depth_norm_gain, depth_norm_shift, mixer_out, late_norm_gain, late_norm_shift, late_up, late_up_bias, late_down, late_down_bias, final_gain, final_shift)
    weights = tuple((item.astype(jnp.float32) for item in listed))
    clips = inputs.astype(jnp.float32).reshape(N_DP, LEN, D)
    flags = slot_flags.astype(jnp.float32)

    def forward(clips, weights):
        e_gain, e_shift, e_up, e_up_bias, e_down, e_down_bias, a_gain, a_shift, q_weight, q_bias, k_weight, v_weight, v_bias, d_table, a_weight, a_bias, m_gain, m_shift, g_weight, d_kernel, d_gain, d_shift, m_out, l_gain, l_shift, l_up, l_up_bias, l_down, l_down_bias, f_gain, f_shift = weights
        table = low(d_table)

        def one_clip(carry, item):
            rows, flag = item
            residual = feed_forward(rows, e_gain, e_shift, e_up, e_up_bias, e_down, e_down_bias)
            residual = attention(residual, a_gain, a_shift, q_weight, q_bias, k_weight, v_weight, v_bias, table, a_weight, a_bias)
            residual = mixer(residual, m_gain, m_shift, g_weight, d_kernel, d_gain, d_shift, m_out)
            residual = feed_forward(residual, l_gain, l_shift, l_up, l_up_bias, l_down, l_down_bias)
            return (carry, flag * layer_norm(residual, f_gain, f_shift))
        return lax.scan(jax.checkpoint(one_clip), jnp.zeros((), jnp.float32), (clips, flags))[1]
    result, pullback = jax.vjp(forward, clips, weights)
    clip_gradient, weight_gradients = pullback(cotangent.astype(jnp.float32).reshape(N_DP, LEN, D))
    g_e_gain, g_e_shift, g_e_up, g_e_up_bias, g_e_down, g_e_down_bias, g_a_gain, g_a_shift, g_q_weight, g_q_bias, g_k_weight, g_v_weight, g_v_bias, g_d_table, g_a_weight, g_a_bias, g_m_gain, g_m_shift, g_g_weight, g_d_kernel, g_d_gain, g_d_shift, g_m_out, g_l_gain, g_l_shift, g_l_up, g_l_up_bias, g_l_down, g_l_down_bias, g_f_gain, g_f_shift = weight_gradients
    return (result.reshape(N_DP * LEN, D).astype(jnp.bfloat16), clip_gradient.reshape(N_DP * LEN, D), g_e_gain, g_e_shift, g_e_up, g_e_up_bias, g_e_down, g_e_down_bias, g_a_gain, g_a_shift, g_q_weight, g_q_bias, g_k_weight, g_v_weight, g_v_bias, g_d_table, g_a_weight, g_a_bias, g_m_gain, g_m_shift, g_g_weight, g_d_kernel, g_d_gain, g_d_shift, g_m_out, g_l_gain, g_l_shift, g_l_up, g_l_up_bias, g_l_down, g_l_down_bias, g_f_gain, g_f_shift)
```

```python
import functools

import jax
import jax.numpy as jnp
from jax import lax
from jax.experimental import pallas as pl
from jax.experimental.pallas import tpu as pltpu
from jax.sharding import PartitionSpec as P

HEAD_DIM = 64
LEFT = 64
RIGHT = 8
REL = LEFT + RIGHT + 1
TILE = 128
HALO = 32
CHUNK = 64
GRANT = 58 << 20
EPS = 1e-05
SHARED = 24
LOW = jnp.bfloat16
F32 = jnp.float32


def dot(left, right, dims=((1,), (0,))):
    return lax.dot_general(left, right, (dims, ((), ())), preferred_element_type=F32)


def dot_t(left, right):
    return dot(left, right, ((1,), (1,)))


def sigmoid(values):
    return 0.5 * jnp.tanh(0.5 * values) + 0.5


def shape(dims, kind):
    return jax.ShapeDtypeStruct(dims, kind)


def whole(dims):
    return pl.BlockSpec(dims, lambda i, *_: (0,) * len(dims))


def first_half(i, count):
    return jnp.minimum(i, count - 1)


def second_half(i, count):
    return jnp.maximum(i - count, 0)


def launch(body, name, grid, operands, specs, outs, out_specs, scratch=(), scalars=(), flops=0):
    moved = sum(item.size * item.dtype.itemsize for item in (*operands, *outs))
    return pl.pallas_call(
        body,
        grid_spec=pltpu.PrefetchScalarGridSpec(
            num_scalar_prefetch=len(scalars),
            grid=grid,
            in_specs=specs,
            out_specs=out_specs,
            scratch_shapes=list(scratch),
        ),
        out_shape=outs,
        compiler_params=pltpu.CompilerParams(
            dimension_semantics=("arbitrary",) * len(grid), vmem_limit_bytes=GRANT
        ),
        cost_estimate=pl.CostEstimate(flops=flops, transcendentals=0, bytes_accessed=moved),
        name=name,
    )(*scalars, *operands)


def normed_rows(values):
    center = values - jnp.mean(values, axis=1, keepdims=True)
    inverse = lax.rsqrt(jnp.mean(center * center, axis=1, keepdims=True) + EPS)
    return center * inverse, inverse


def row_loop(rows, body, initial=0):
    def step(i, carry):
        return body(pl.ds(pl.multiple_of(i * CHUNK, CHUNK), CHUNK), carry)

    return lax.fori_loop(0, rows // CHUNK, step, initial)


def norm_into(source, gain, shift, target):
    def rows(at, carry):
        hat, _ = normed_rows(source[at, :].astype(F32))
        target[at, :] = (hat * gain[...] + shift[...]).astype(LOW)
        return carry

    row_loop(source.shape[0], rows)


def fold(values):
    return jnp.sum(values.reshape(values.shape[0] // 8, 8, values.shape[1]), axis=0)


def norm_back(upstream, values, gain):
    hat, inverse = normed_rows(values)
    scaled = upstream * gain
    first = jnp.mean(scaled, axis=1, keepdims=True)
    second = jnp.mean(scaled * hat, axis=1, keepdims=True)
    return inverse * (scaled - first - hat * second), hat


def feed_kernel(x, gain, shift, up0, up1, bias0, bias1, down0, down1, bias, n, s0, s1, a0, a1, out):
    i = pl.program_id(0)
    count = pl.num_programs(0) // 2

    @pl.when(i == 0)
    def _():
        norm_into(x, gain, shift, n)

    def part(up, up_bias, down, slope, active, start):
        hidden = dot(n[...], up[...]) + up_bias[...]
        gate = sigmoid(hidden)
        swished = hidden * gate
        slope[...] = (gate + swished * (1.0 - gate)).astype(LOW)
        low = swished.astype(LOW)
        active[...] = low
        product = dot(low, down[...])
        if start:
            out[...] = product
        else:
            out[...] += product

    pl.when(i == 0)(lambda: part(up0, bias0, down0, s0, a0, True))
    pl.when((i > 0) & (i < count))(lambda: part(up0, bias0, down0, s0, a0, False))
    pl.when(i >= count)(lambda: part(up1, bias1, down1, s1, a1, False))

    @pl.when(i == 2 * count - 1)
    def _():
        def rows(at, carry):
            out[at, :] = x[at, :].astype(F32) + 0.5 * (out[at, :] + bias[...])
            return carry

        row_loop(x.shape[0], rows)


def feed_forward(x, gain, shift, up, up_bias, down, bias):
    rows, width = x.shape
    hidden = up[0].shape[1]
    tile = min(512, hidden)
    count = hidden // tile
    own = functools.partial(first_half, count=count)
    oth = functools.partial(second_half, count=count)
    column = lambda height, pick: pl.BlockSpec((height, tile), lambda i: (0, pick(i)))
    row = lambda pick: pl.BlockSpec((tile, width), lambda i: (pick(i), 0))
    return launch(
        feed_kernel,
        "feed_forward",
        (2 * count,),
        (x, gain, shift, *up, *up_bias, *down, bias),
        [
            whole((rows, width)),
            whole((1, width)),
            whole((1, width)),
            column(width, own),
            column(width, oth),
            column(1, own),
            column(1, oth),
            row(own),
            row(oth),
            whole((1, width)),
        ],
        [shape((rows, width), LOW)] + [shape((rows, hidden), LOW)] * 4 + [shape((rows, width), F32)],
        [
            whole((rows, width)),
            column(rows, own),
            column(rows, oth),
            column(rows, own),
            column(rows, oth),
            whole((rows, width)),
        ],
        flops=8 * rows * width * hidden,
    )


def feed_half_kernel(first, x, *refs):
    i = pl.program_id(0)
    if first:
        gain, shift, up, up_bias, down, n, slope, active, out = refs
        pl.when(i == 0)(lambda: norm_into(x, gain, shift, n))
    else:
        n, prior, bias, up, up_bias, down, slope, active, out = refs
    hidden = dot(n[...], up[...]) + up_bias[...]
    gate = sigmoid(hidden)
    swished = hidden * gate
    slope[...] = (gate + swished * (1.0 - gate)).astype(LOW)
    low = swished.astype(LOW)
    active[...] = low
    product = dot(low, down[...])

    @pl.when(i == 0)
    def _():
        out[...] = product if first else prior[...] + product

    @pl.when(i > 0)
    def _():
        out[...] += product

    if not first:
        @pl.when(i == pl.num_programs(0) - 1)
        def _():
            def rows(at, carry):
                out[at, :] = x[at, :].astype(F32) + 0.5 * (out[at, :] + bias[...])
                return carry

            row_loop(x.shape[0], rows)


def feed_half(first, x, extra, up, up_bias, down):
    rows, width = x.shape
    hidden = up.shape[1]
    tile = min(512, hidden)
    column = lambda height: pl.BlockSpec((height, tile), lambda i: (0, i))
    outs = [shape((rows, width), LOW)] * first
    outs += [shape((rows, hidden), LOW)] * 2 + [shape((rows, width), F32)]
    return launch(
        functools.partial(feed_half_kernel, first),
        "feed_half",
        (hidden // tile,),
        (x, *extra, up, up_bias, down),
        [whole(item.shape) for item in (x, *extra)]
        + [column(width), column(1), pl.BlockSpec((tile, width), lambda i: (i, 0))],
        outs,
        [whole((rows, width))] * first + [column(rows), column(rows), whole((rows, width))],
        flops=4 * rows * width * hidden,
    )


def feed_back_kernel(scale, g, d, x, gain, up0, up1, down0, down1, s0, s1, k0, k1, t0, t1, out, *rest):
    i = pl.program_id(0)
    count = pl.num_programs(0) // 2
    low, sums, total = rest if scale else (None, *rest)

    def part(up, down, slope, key, tally, start):
        back = dot_t(d[...], down[...]) * slope[...].astype(F32)
        key_low = back.astype(LOW)
        key[...] = key_low
        tally[...] = dot(jnp.ones((8, key_low.shape[0]), LOW), key_low)
        product = dot_t(key_low, up[...])
        if start:
            total[...] = product
        else:
            total[...] += product

    pl.when(i == 0)(lambda: part(up0, down0, s0, k0, t0, True))
    pl.when((i > 0) & (i < count))(lambda: part(up0, down0, s0, k0, t0, False))
    pl.when(i >= count)(lambda: part(up1, down1, s1, k1, t1, False))

    @pl.when(i == 2 * count - 1)
    def _():
        def rows(at, carry):
            upstream = total[at, :]
            change, hat = norm_back(upstream, x[at, :].astype(F32), gain[...])
            gradient = g[at, :] + change
            out[at, :] = gradient
            if scale:
                low[at, :] = (scale * gradient).astype(LOW)
            return (
                carry[0] + fold(upstream * hat),
                carry[1] + fold(upstream),
                carry[2] + fold(d[at, :].astype(F32)),
            )

        zero = jnp.zeros((8, x.shape[1]), F32)
        first, second, third = row_loop(x.shape[0], rows, (zero, zero, zero))
        sums[0:8, :] = first
        sums[8:16, :] = second
        sums[16:24, :] = third


def feed_back(scale, g, d, x, gain, up, down, slope):
    rows, width = x.shape
    hidden = up[0].shape[1]
    tile = min(512, hidden)
    count = hidden // tile
    own = functools.partial(first_half, count=count)
    oth = functools.partial(second_half, count=count)
    column = lambda height, pick: pl.BlockSpec((height, tile), lambda i: (0, pick(i)))
    row = lambda pick: pl.BlockSpec((tile, width), lambda i: (pick(i), 0))
    outs = [shape((rows, hidden), LOW)] * 2 + [shape((8, hidden), F32)] * 2
    outs += [shape((rows, width), F32)] + [shape((rows, width), LOW)] * bool(scale)
    outs += [shape((24, width), F32)]
    return launch(
        functools.partial(feed_back_kernel, scale),
        "feed_back",
        (2 * count,),
        (g, d, x, gain, *up, *down, *slope),
        [
            whole((rows, width)),
            whole((rows, width)),
            whole((rows, width)),
            whole((1, width)),
            column(width, own),
            column(width, oth),
            row(own),
            row(oth),
            column(rows, own),
            column(rows, oth),
        ],
        outs,
        [column(rows, own), column(rows, oth), column(8, own), column(8, oth)]
        + [whole((rows, width))] * (1 + bool(scale))
        + [whole((24, width))],
        scratch=[pltpu.VMEM((rows, width), F32)],
        flops=8 * rows * width * hidden,
    )


def feed_key_kernel(d, down0, down1, s0, s1, k0, k1, t0, t1):
    i = pl.program_id(0)
    count = pl.num_programs(0) // 2

    def part(down, slope, key, tally):
        low = (dot_t(d[...], down[...]) * slope[...].astype(F32)).astype(LOW)
        key[...] = low
        tally[...] = dot(jnp.ones((8, low.shape[0]), LOW), low)

    pl.when(i < count)(lambda: part(down0, s0, k0, t0))
    pl.when(i >= count)(lambda: part(down1, s1, k1, t1))


def feed_key(d, down, slope):
    rows, width = d.shape
    hidden = slope[0].shape[1]
    tile = min(512, hidden)
    count = hidden // tile
    own = functools.partial(first_half, count=count)
    oth = functools.partial(second_half, count=count)
    column = lambda height, pick: pl.BlockSpec((height, tile), lambda i: (0, pick(i)))
    row = lambda pick: pl.BlockSpec((tile, width), lambda i: (pick(i), 0))
    return launch(
        feed_key_kernel,
        "feed_key",
        (2 * count,),
        (d, *down, *slope),
        [whole((rows, width)), row(own), row(oth), column(rows, own), column(rows, oth)],
        [shape((rows, hidden), LOW)] * 2 + [shape((8, hidden), F32)] * 2,
        [column(rows, own), column(rows, oth), column(8, own), column(8, oth)],
        flops=4 * rows * width * hidden,
    )


def feed_end_kernel(g, d, x, gain, up0, up1, k0, k1, out, sums, total):
    i = pl.program_id(0)
    count = pl.num_programs(0) // 2

    def part(up, key, start):
        product = dot_t(key[...], up[...])
        if start:
            total[...] = product
        else:
            total[...] += product

    pl.when(i == 0)(lambda: part(up0, k0, True))
    pl.when((i > 0) & (i < count))(lambda: part(up0, k0, False))
    pl.when(i >= count)(lambda: part(up1, k1, False))

    @pl.when(i == 2 * count - 1)
    def _():
        def rows(at, carry):
            upstream = total[at, :]
            change, hat = norm_back(upstream, x[at, :].astype(F32), gain[...])
            out[at, :] = g[at, :] + change
            return (
                carry[0] + fold(upstream * hat),
                carry[1] + fold(upstream),
                carry[2] + fold(d[at, :].astype(F32)),
            )

        zero = jnp.zeros((8, x.shape[1]), F32)
        first, second, third = row_loop(x.shape[0], rows, (zero, zero, zero))
        sums[0:8, :] = first
        sums[8:16, :] = second
        sums[16:24, :] = third


def feed_end(g, d, x, gain, up, key):
    rows, width = x.shape
    hidden = key[0].shape[1]
    tile = min(512, hidden)
    count = hidden // tile
    own = functools.partial(first_half, count=count)
    oth = functools.partial(second_half, count=count)
    column = lambda height, pick: pl.BlockSpec((height, tile), lambda i: (0, pick(i)))
    wide = whole((rows, width))
    return launch(
        feed_end_kernel,
        "feed_end",
        (2 * count,),
        (g, d, x, gain, *up, *key),
        [wide, wide, wide, whole((1, width))]
        + [column(width, own), column(width, oth), column(rows, own), column(rows, oth)],
        [shape((rows, width), F32), shape((24, width), F32)],
        [wide, whole((24, width))],
        scratch=[pltpu.VMEM((rows, width), F32)],
        flops=4 * rows * width * hidden,
    )


def final_kernel(flag, x, cotangent, gain, shift, out, gradient, low, sums):
    live = flag[0].astype(F32)

    @pl.when(pl.program_id(0) == 0)
    def _():
        sums[...] = jnp.zeros_like(sums)

    hat, inverse = normed_rows(x[...])
    out[...] = (live * (hat * gain[...] + shift[...])).astype(LOW)
    upstream = live * cotangent[...].astype(F32)
    scaled = upstream * gain[...]
    first = jnp.mean(scaled, axis=1, keepdims=True)
    second = jnp.mean(scaled * hat, axis=1, keepdims=True)
    change = inverse * (scaled - first - hat * second)
    gradient[...] = change
    low[...] = (0.5 * change).astype(LOW)
    sums[0:8, :] += fold(upstream * hat)
    sums[8:16, :] += fold(upstream)


def final_norm(flag, x, cotangent, gain, shift):
    rows, width = x.shape
    step = min(128, rows)
    block = pl.BlockSpec((step, width), lambda i, *_: (i, 0))
    return launch(
        final_kernel,
        "final_norm",
        (rows // step,),
        (x, cotangent, gain, shift),
        [block, block, whole((1, width)), whole((1, width))],
        [shape((rows, width), LOW), shape((rows, width), F32), shape((rows, width), LOW), shape((16, width), F32)],
        [block, block, block, whole((16, width))],
        scalars=(flag,),
    )


def project_kernel(x, gain, shift, kw0, kw1, vw0, vw1, vb, n, kv):
    i = pl.program_id(0)
    step = kw0.shape[1]
    width = x.shape[1]
    half = width // 2

    @pl.when(i == 0)
    def _():
        norm_into(x, gain, shift, n)

    for side, (kw, vw) in enumerate(((kw0, vw0), (kw1, vw1))):
        at = pl.ds(pl.multiple_of(side * half + i * step, step), step)
        to = pl.ds(pl.multiple_of(width + side * half + i * step, step), step)
        kv[:, at] = dot(n[...], kw[...]).astype(LOW)
        kv[:, to] = (dot(n[...], vw[...]) + vb[:, at]).astype(LOW)


def project(x, gain, shift, kw, vw, vb):
    rows, width = x.shape
    half = width // 2
    step = 256
    weight = pl.BlockSpec((width, step), lambda i: (0, i))
    thin = whole((1, width))
    return launch(
        project_kernel,
        "project",
        (half // step,),
        (x, gain, shift, *kw, *vw, vb),
        [whole((rows, width)), thin, thin] + [weight] * 4 + [thin],
        [shape((rows, width), LOW), shape((rows, 2 * width), LOW)],
        [whole((rows, width)), whole((rows, 2 * width))],
        flops=4 * rows * width * width,
    )


def query_kernel(n, qw0, qw1, qb, q):
    i = pl.program_id(0)
    step = qw0.shape[1]
    half = q.shape[1] // 2
    for side, qw in enumerate((qw0, qw1)):
        at = pl.ds(pl.multiple_of(side * half + i * step, step), step)
        q[:, at] = ((dot(n[...], qw[...]) + qb[:, at]).astype(LOW).astype(F32) * HEAD_DIM**-0.5).astype(LOW)


def query(n, qw, qb):
    rows, width = n.shape
    half = width // 2
    step = 256
    weight = pl.BlockSpec((width, step), lambda i: (0, i))
    wide = whole((rows, width))
    return launch(
        query_kernel,
        "query",
        (half // step,),
        (n, *qw, qb),
        [wide, weight, weight, whole((1, width))],
        [shape((rows, width), LOW)],
        [wide],
        flops=2 * rows * width * width,
    )[0]


def in_head(head, dims):
    return (lax.broadcasted_iota(jnp.int32, dims, 1) // HEAD_DIM) == head


def band_of(block):
    rows = block.shape[0]
    left = jnp.broadcast_to(block[:, 0:1], (rows, TILE))
    right = jnp.broadcast_to(block[:, TILE - 1 : TILE], (rows, TILE))
    lane = lax.broadcasted_iota(jnp.int32, (rows, TILE), 1)
    mixed = jnp.where(lane < TILE // 2, right, left)
    spread = jnp.concatenate([block, right, mixed, left], axis=1)
    band = pltpu.roll(spread, LEFT, 1, stride=1, stride_axis=0)
    return left, right, [band[:, t * TILE : (t + 1) * TILE] for t in range(3)]


def attend_kernel(core, q, k0, v0, k1, v1, table, o, lse, prob, scores):
    rows = q.shape[0]
    blocks = rows // TILE
    second = core[0] == 1
    mixed = []
    peaks = []
    for head in range(2):
        inside = in_head(head, q.shape)
        query = jnp.where(inside, q[...], jnp.zeros_like(q))
        scores[:, :rows] = dot_t(query, k0[...])
        scores[:, rows:] = dot_t(query, k1[...])
        relative = dot_t(query, table[...])
        totals = []
        for b in range(blocks):
            at = slice(b * TILE, (b + 1) * TILE)
            left, right, band = band_of(relative[at, :])
            far = jnp.where(second, left, right)
            tiles = []
            for t in range(blocks):
                gap = t - b
                term = left if gap <= -2 else right if gap >= 2 else band[gap + 1]
                tiles.append(scores[at, t * TILE : (t + 1) * TILE] + term)
            for t in range(blocks):
                term = far
                if b == blocks - 1 and t == 0:
                    term = jnp.where(second, left, band[2])
                if b == 0 and t == blocks - 1:
                    term = jnp.where(second, band[0], right)
                tiles.append(scores[at, rows + t * TILE : rows + (t + 1) * TILE] + term)
            peak = functools.reduce(jnp.maximum, tiles)
            peak = jnp.max(peak, axis=1, keepdims=True)
            total = jnp.zeros((TILE, TILE), F32)
            for t, tile in enumerate(tiles):
                value = jnp.exp(tile - peak)
                total = total + value
                prob[at, t * TILE : (t + 1) * TILE] = value.astype(LOW)
            total = jnp.sum(total, axis=1, keepdims=True)
            totals.append((peak, total))
        product = dot(prob[:, :rows], v0[...]) + dot(prob[:, rows:], v1[...])
        mixed.append(
            jnp.concatenate(
                [
                    product[b * TILE : (b + 1) * TILE] * (1.0 / totals[b][1])
                    for b in range(blocks)
                ],
                axis=0,
            )
        )
        peaks.append(jnp.concatenate([peak + jnp.log(total) for peak, total in totals], axis=0))
    o[0] = jnp.where(in_head(0, q.shape), mixed[0], mixed[1]).astype(LOW)
    lane = lax.broadcasted_iota(jnp.int32, (rows, TILE), 1)
    columns = jnp.where(lane == 0, peaks[0], jnp.where(lane == 1, peaks[1], 0.0))
    lse[...] = jnp.transpose(columns)[0:8, :]


def pair_specs(rows, pairs, start):
    near = pl.BlockSpec((rows, TILE), lambda i, *_: (0, start + i))
    near_value = pl.BlockSpec((rows, TILE), lambda i, *_: (0, pairs + start + i))
    far = pl.BlockSpec((rows, TILE), lambda i, *_: (0, (start + i + pairs // 2) % pairs))
    far_value = pl.BlockSpec((rows, TILE), lambda i, *_: (0, pairs + (start + i + pairs // 2) % pairs))
    return [near, near_value, far, far_value]


def attend(core, q, kv, kvr, table):
    rows, width = q.shape
    pairs = width // TILE
    specs = pair_specs(rows, pairs, 0)
    count = pairs // 2
    joined = pl.BlockSpec((1, rows, TILE), lambda i, *_: (i // count, 0, i % count))
    return launch(
        attend_kernel,
        "attend",
        (pairs,),
        (q, kv, kv, kvr, kvr, table),
        [specs[0], *specs, whole((TILE, TILE))],
        [shape((2, rows, width // 2), LOW), shape((8 * pairs, rows), F32)],
        [joined, pl.BlockSpec((8, rows), lambda i, *_: (i, 0))],
        scratch=[pltpu.VMEM((rows, 2 * rows), LOW), pltpu.VMEM((rows, 2 * rows), F32)],
        scalars=(core,),
        flops=8 * rows * rows * width,
    )


def attend_back_kernel(
    core, q, do, o, k0, v0, k1, v1, table, lse, kq, dk0, dv0, dkv1, dtable, prob, slope, scores, ds_back, de
):
    rows = q.shape[0]
    blocks = rows // TILE
    second = core[0] == 1

    @pl.when(pl.program_id(0) == 0)
    def _():
        dtable[...] = jnp.zeros_like(dtable)

    lane = lax.broadcasted_iota(jnp.int32, (TILE, TILE), 1)
    sub = lax.broadcasted_iota(jnp.int32, (TILE, TILE), 0)
    flip = jnp.where(lane + sub == TILE - 1, 1.0, 0.0).astype(LOW)
    keys_t = [jnp.transpose(ref[...].astype(F32)).astype(LOW) for ref in (k0, k1)]
    table_t = jnp.transpose(table[...].astype(F32)).astype(LOW)
    product = do[...].astype(F32) * o[0].astype(F32)
    pieces = []
    gq = []
    for head in range(2):
        inside = in_head(head, q.shape)
        zero = jnp.zeros_like(q)
        query = jnp.where(inside, q[...], zero)
        upstream = jnp.where(inside, do[...], zero)
        ones = jnp.where(in_head(head, (8, TILE)), 1.0, 0.0).astype(F32)
        delta = lax.dot_general(
            ones, product, (((1,), (1,)), ((), ())), precision=lax.Precision.HIGHEST, preferred_element_type=F32
        )[0:1, :]
        level = lse[head : head + 1, :]
        relative = dot_t(query, table[...])
        ends = dot_t(jnp.concatenate([table[0:8, :], table[TILE - 8 :, :]], axis=0), query)
        left_end = ends[0:1, :] - level
        right_end = ends[15:16, :] - level
        far_end = jnp.where(second, left_end, right_end)
        scores[:rows, :] = dot_t(k0[...], query)
        scores[rows:, :] = dot_t(k1[...], query)
        ds_back[:rows, :] = dot_t(v0[...], upstream)
        ds_back[rows:, :] = dot_t(v1[...], upstream)
        for b in range(blocks):
            at = slice(b * TILE, (b + 1) * TILE)
            _, _, band = band_of(relative[at, :])
            turned = [jnp.transpose(item) - level[:, at] for item in band]
            kept = {}
            for t in range(2 * blocks):
                down = slice(t * TILE, (t + 1) * TILE)
                gap = t - b
                if t < blocks:
                    if gap <= -2:
                        term = left_end[:, at]
                    elif gap >= 2:
                        term = right_end[:, at]
                    else:
                        term = turned[gap + 1]
                else:
                    term = far_end[:, at]
                    if b == blocks - 1 and t == blocks:
                        term = jnp.where(second, jnp.broadcast_to(left_end[:, at], (TILE, TILE)), turned[2])
                    if b == 0 and t == 2 * blocks - 1:
                        term = jnp.where(second, turned[0], jnp.broadcast_to(right_end[:, at], (TILE, TILE)))
                value = jnp.exp(scores[down, at] + term)
                prob[down, at] = value.astype(LOW)
                change = (value * (ds_back[down, at] - delta[:, at])).astype(LOW)
                slope[down, at] = change
                if t < blocks and abs(gap) <= 1:
                    kept[gap + 1] = change
                if b == blocks - 1 and t == blocks:
                    kept[2] = jnp.where(second, jnp.zeros_like(change), change)
                if b == 0 and t == 2 * blocks - 1:
                    kept[0] = jnp.where(second, change, jnp.zeros_like(change))
            stretched = jnp.concatenate([dot_t(flip, kept[g]) for g in range(3)] + [jnp.zeros((TILE, TILE), F32)], axis=1)
            back = pltpu.roll(stretched, 3 * TILE + 1 - LEFT, 1, stride=1, stride_axis=0)
            tiles = [back[:, t * TILE : (t + 1) * TILE] for t in range(4)]
            right_sum = tiles[1] + jnp.where(lane < TILE // 2, tiles[2], 0.0)
            left_sum = tiles[3] + jnp.where(lane < TILE // 2, 0.0, tiles[2])
            right_sum = jnp.sum(right_sum, axis=1, keepdims=True)
            left_sum = jnp.sum(left_sum, axis=1, keepdims=True)
            full = tiles[0] + jnp.where(lane == 0, left_sum, 0.0) + jnp.where(lane == TILE - 1, right_sum, 0.0)
            de[:, at] = dot(jnp.transpose(full).astype(LOW), flip)
        here = slice(head * HEAD_DIM, (head + 1) * HEAD_DIM)
        sums = [0.0, 0.0]
        gradient = 0.0
        for side in range(2):
            column = lax.broadcasted_iota(jnp.int32, (16, rows), 1) // TILE
            row = lax.broadcasted_iota(jnp.int32, (16, rows), 0)
            marks = jnp.where(column == row, 1.0, 0.0).astype(LOW)
            mixed = dot(
                jnp.concatenate([keys_t[side][here, :], marks], axis=0),
                slope[side * rows : (side + 1) * rows, :],
            )
            gradient = gradient + mixed[:HEAD_DIM]
            sums[side] = mixed[HEAD_DIM : HEAD_DIM + 8]
        position = lax.broadcasted_iota(jnp.int32, (8, rows), 1) // TILE
        tile_row = lax.broadcasted_iota(jnp.int32, (8, rows), 0)
        gap = tile_row - position
        left_add = jnp.where((gap <= -2) & (tile_row < blocks), sums[0], 0.0)
        right_add = jnp.where((gap >= 2) & (tile_row < blocks), sums[0], 0.0)
        others = jnp.where(tile_row < blocks, sums[1], 0.0)
        left_other = jnp.where((position == 0) & (tile_row == blocks - 1), 0.0, others)
        right_other = jnp.where((position == blocks - 1) & (tile_row == 0), 0.0, others)
        left_add = left_add + jnp.where(second, left_other, 0.0)
        right_add = right_add + jnp.where(second, 0.0, right_other)
        left_add = jnp.sum(left_add, axis=0, keepdims=True)
        right_add = jnp.sum(right_add, axis=0, keepdims=True)
        where = lax.broadcasted_iota(jnp.int32, (TILE, rows), 0)
        de_low = (
            de[...] + jnp.where(where == 0, left_add, 0.0) + jnp.where(where == TILE - 1, right_add, 0.0)
        ).astype(LOW)
        gradient = gradient + dot(table_t[here, :], de_low)
        gq.append(gradient)
        pieces.append(
            (
                dot(slope[:rows, :], q[...]),
                dot(prob[:rows, :], do[...]),
                dot(slope[rows:, :], q[...]),
                dot(prob[rows:, :], do[...]),
                dot(de_low, q[...]),
            )
        )
    turned = jnp.transpose(jnp.concatenate(gq, axis=0))
    kq[...] = (turned * HEAD_DIM**-0.5).astype(LOW)
    chosen = in_head(0, q.shape)
    dk0[...] = jnp.where(chosen, pieces[0][0], pieces[1][0])
    dv0[...] = jnp.where(chosen, pieces[0][1], pieces[1][1])
    dkv1[0] = jnp.where(chosen, pieces[0][2], pieces[1][2]).astype(LOW)
    dkv1[1] = jnp.where(chosen, pieces[0][3], pieces[1][3]).astype(LOW)
    dtable[...] += jnp.where(in_head(0, (TILE, TILE)), pieces[0][4], pieces[1][4])


def attend_back(core, start, q, do, o, kv, kvr, table, lse):
    rows, width = q.shape
    pairs = width // TILE
    half = width // 2
    specs = pair_specs(rows, pairs, start)
    near = pl.BlockSpec((rows, TILE), lambda i, *_: (0, i))
    square = whole((TILE, TILE))
    return launch(
        attend_back_kernel,
        "attend_back",
        (pairs // 2,),
        (q, do, o, kv, kv, kvr, kvr, table, lse),
        [
            specs[0],
            near,
            pl.BlockSpec((1, rows, TILE), lambda i, *_: (start // (pairs // 2), 0, i)),
            *specs,
            square,
            pl.BlockSpec((8, rows), lambda i, *_: (start + i, 0)),
        ],
        [
            shape((rows, half), LOW),
            shape((rows, half), F32),
            shape((rows, half), F32),
            shape((2, rows, half), LOW),
            shape((TILE, TILE), F32),
        ],
        [near, near, near, pl.BlockSpec((2, rows, TILE), lambda i, *_: (0, 0, i)), square],
        scratch=[
            pltpu.VMEM((2 * rows, rows), LOW),
            pltpu.VMEM((2 * rows, rows), LOW),
            pltpu.VMEM((2 * rows, rows), F32),
            pltpu.VMEM((2 * rows, rows), F32),
            pltpu.VMEM((TILE, rows), F32),
        ],
        scalars=(core,),
        flops=10 * rows * rows * width,
    )


def mixer_in_kernel(o0, o1, x, out0, out1, bias, gain, shift, lin0, gate0, lin1, gate1, x2, n, u, sig, edge):
    i = pl.program_id(0)
    count = pl.num_programs(0) // 2

    @pl.when(i == 0)
    def _():
        x2[...] = x[...] + (dot(o0[0], out0[...]) + dot(o1[0], out1[...]) + bias[...])
        norm_into(x2, gain, shift, n)

    def part(lin, gate):
        value = sigmoid(dot(n[...], gate[0]))
        sig[...] = value
        product = dot(n[...], lin[0]) * value
        u[...] = product
        edge[...] = product[product.shape[0] - HALO :]

    pl.when(i < count)(lambda: part(lin0, gate0))
    pl.when(i >= count)(lambda: part(lin1, gate1))


def mixer_in(o, x, out, bias, gain, shift, gated):
    rows, width = x.shape
    half = width // 2
    tile = 256
    count = half // tile
    wide, thin = whole((rows, width)), whole((1, width))
    pick = lambda index, side: pl.BlockSpec(
        (1, width, tile), lambda i: (index, 0, side(i, count))
    )
    column = pl.BlockSpec((rows, tile), lambda i: (0, i))
    return launch(
        mixer_in_kernel,
        "mixer_in",
        (2 * count,),
        (o, o, x, *out, bias, gain, shift, gated[0], gated[0], gated[1], gated[1]),
        [
            pl.BlockSpec((1, rows, half), lambda i: (0, 0, 0)),
            pl.BlockSpec((1, rows, half), lambda i: (1, 0, 0)),
            wide,
            whole((half, width)),
            whole((half, width)),
            thin,
            thin,
            thin,
            pick(0, first_half),
            pick(1, first_half),
            pick(0, second_half),
            pick(1, second_half),
        ],
        [
            shape((rows, width), F32),
            shape((rows, width), LOW),
            shape((rows, width), F32),
            shape((rows, width), F32),
            shape((HALO, width), F32),
        ],
        [
            wide,
            wide,
            column,
            column,
            pl.BlockSpec((HALO, tile), lambda i: (0, (i + count) % (2 * count))),
        ],
        flops=6 * rows * width * width,
    )


def mixer_out_kernel(u, edge, kernel, gain, shift, out0, out1, x2, z, w0, w1, x3, held):
    i = pl.program_id(0)
    rows = u.shape[0]
    taps = kernel.shape[0] - 1
    held[:HALO, :] = edge[...]
    held[HALO:, :] = u[...]
    at = pl.ds(pl.multiple_of(i * TILE, TILE), TILE)
    for start in range(0, rows, CHUNK):
        total = jnp.zeros((CHUNK, TILE), F32)
        for k in range(taps):
            begin = start + k + HALO + 1 - taps
            total = total + kernel[k : k + 1, :] * held[begin : begin + CHUNK, :]
        z[start : start + CHUNK, at] = total

    @pl.when(i == pl.num_programs(0) - 1)
    def _():
        half = out0.shape[0]

        def step(rows_at, carry):
            hat, _ = normed_rows(z[rows_at, :])
            y = hat * gain[...] + shift[...]
            w = (y * sigmoid(y)).astype(LOW)
            w0[rows_at, :] = w[:, :half]
            w1[rows_at, :] = w[:, half:]
            return carry

        row_loop(rows, step)
        x3[...] = x2[...] + (dot(w0[...], out0[...]) + dot(w1[...], out1[...]))


def mixer_out(u, edge, kernel, gain, shift, out, x2):
    rows, width = u.shape
    half = width // 2
    wide, thin = whole((rows, width)), whole((1, width))
    column = lambda height: pl.BlockSpec((height, TILE), lambda i: (0, i))
    return launch(
        mixer_out_kernel,
        "mixer_out",
        (width // TILE,),
        (u, edge, kernel, gain, shift, *out, x2),
        [column(rows), column(HALO), column(kernel.shape[0]), thin, thin]
        + [whole((half, width))] * 2
        + [wide],
        [shape((rows, width), F32)] + [shape((rows, half), LOW)] * 2 + [shape((rows, width), F32)],
        [wide] + [whole((rows, half))] * 2 + [wide],
        scratch=[pltpu.VMEM((rows + HALO, TILE), F32)],
        flops=2 * rows * width * width,
    )


def mixer_mid_kernel(d, out0, out1, z, gain, shift, bz, sums, head):
    half = out0.shape[0]
    rows = d.shape[0]
    bz[:, :half] = dot_t(d[...], out0[...])
    bz[:, half:] = dot_t(d[...], out1[...])

    def step(at, carry):
        hat, inverse = normed_rows(z[at, :])
        y = hat * gain[...] + shift[...]
        gate = sigmoid(y)
        upstream = bz[at, :] * (gate + y * gate * (1.0 - gate))
        scaled = upstream * gain[...]
        first = jnp.mean(scaled, axis=1, keepdims=True)
        second = jnp.mean(scaled * hat, axis=1, keepdims=True)
        bz[at, :] = inverse * (scaled - first - hat * second)
        return carry[0] + fold(upstream * hat), carry[1] + fold(upstream)

    zero = jnp.zeros((8, d.shape[1]), F32)
    first, second = row_loop(rows, step, (zero, zero))
    sums[0:8, :] = first
    sums[8:16, :] = second
    head[:, half:] = bz[:HALO, :half]
    head[:, :half] = bz[:HALO, half:]


def mixer_mid(d, out, z, gain, shift):
    rows, width = d.shape
    half = width // 2
    wide, thin = whole((rows, width)), whole((1, width))
    return launch(
        mixer_mid_kernel,
        "mixer_mid",
        (1,),
        (d, *out, z, gain, shift),
        [wide, whole((half, width)), whole((half, width)), wide, thin, thin],
        [shape((rows, width), F32), shape((16, width), F32), shape((HALO, width), F32)],
        [wide, whole((16, width)), whole((HALO, width))],
        flops=2 * rows * width * width,
    )


def mixer_back_kernel(
    bz, tail, u, edge, kernel, sig, lin0, gate0, lin1, gate1, x2, gain, g, out0, out1,
    own, oth, dkernel, gradient, low, do0, do1, sums, held, later, total, taps_sum, keys,
):
    i = pl.program_id(0)
    count = pl.num_programs(0) // 2
    rows = u.shape[0]
    taps = kernel.shape[0] - 1
    held[:HALO, :] = edge[...]
    held[HALO:, :] = u[...]
    later[:rows, :] = bz[...]
    later[rows:, :] = tail[...]
    taps_sum[...] = jnp.zeros_like(taps_sum)
    for start in range(0, rows, CHUNK):
        here = slice(start, start + CHUNK)
        upstream = later[here, :]
        change = jnp.zeros((CHUNK, TILE), F32)
        for k in range(taps):
            ahead = start + taps - 1 - k
            change = change + kernel[k : k + 1, :] * later[ahead : ahead + CHUNK, :]
            begin = start + k + HALO + 1 - taps
            taps_sum[8 * k : 8 * k + 8, :] += fold(upstream * held[begin : begin + CHUNK, :])
        gate = sig[here, :]
        linear = change * gate
        keys[here, :TILE] = linear.astype(LOW)
        keys[here, TILE:] = (change * held[start + HALO : start + HALO + CHUNK, :] * (1.0 - gate)).astype(LOW)
    dkernel[...] = jnp.sum(taps_sum[...].reshape(kernel.shape[0], 8, TILE), axis=1)

    def part(lin, gate, target, start):
        target[0] = keys[:, :TILE]
        target[1] = keys[:, TILE:]
        product = dot_t(keys[...], jnp.concatenate([lin[0], gate[0]], axis=1))
        if start:
            total[...] = product
        else:
            total[...] += product

    pl.when(i == 0)(lambda: part(lin0, gate0, own, True))
    pl.when((i > 0) & (i < count))(lambda: part(lin0, gate0, own, False))
    pl.when(i >= count)(lambda: part(lin1, gate1, oth, False))

    @pl.when(i == pl.num_programs(0) - 1)
    def _():
        def step(at, carry):
            upstream = total[at, :]
            change, hat = norm_back(upstream, x2[at, :], gain[...])
            value = g[at, :] + change
            gradient[at, :] = value
            rounded = value.astype(LOW)
            low[at, :] = rounded
            return (
                carry[0] + fold(upstream * hat),
                carry[1] + fold(upstream),
                carry[2] + fold(rounded.astype(F32)),
            )

        zero = jnp.zeros((8, x2.shape[1]), F32)
        first, second, third = row_loop(rows, step, (zero, zero, zero))
        sums[0:8, :] = first
        sums[8:16, :] = second
        sums[16:24, :] = third
        do0[...] = dot_t(low[...], out0[...]).astype(LOW)
        do1[...] = dot_t(low[...], out1[...]).astype(LOW)


def mixer_back(bz, tail, u, edge, kernel, sig, gated, x2, gain, g, out):
    rows, width = u.shape
    half = width // 2
    count = half // TILE
    wide, thin = whole((rows, width)), whole((1, width))
    column = lambda height: pl.BlockSpec((height, TILE), lambda i: (0, i))
    pick = lambda index, side: pl.BlockSpec(
        (1, width, TILE), lambda i: (index, 0, side(i, count))
    )
    return launch(
        mixer_back_kernel,
        "mixer_back",
        (2 * count,),
        (bz, tail, u, edge, kernel, sig, gated[0], gated[0], gated[1], gated[1], x2, gain, g, *out),
        [
            column(rows),
            column(HALO),
            column(rows),
            column(HALO),
            column(kernel.shape[0]),
            column(rows),
            pick(0, first_half),
            pick(1, first_half),
            pick(0, second_half),
            pick(1, second_half),
            wide,
            thin,
            wide,
            whole((half, width)),
            whole((half, width)),
        ],
        [
            shape((2, rows, half), LOW),
            shape((2, rows, half), LOW),
            shape(kernel.shape, F32),
            shape((rows, width), F32),
            shape((rows, width), LOW),
            shape((rows, half), LOW),
            shape((rows, half), LOW),
            shape((24, width), F32),
        ],
        [
            pl.BlockSpec((2, rows, TILE), lambda i: (0, 0, first_half(i, count))),
            pl.BlockSpec((2, rows, TILE), lambda i: (0, 0, second_half(i, count))),
            column(kernel.shape[0]),
            wide,
            wide,
            whole((rows, half)),
            whole((rows, half)),
            whole((24, width)),
        ],
        scratch=[
            pltpu.VMEM((rows + HALO, TILE), F32),
            pltpu.VMEM((rows + HALO, TILE), F32),
            pltpu.VMEM((rows, width), F32),
            pltpu.VMEM((8 * kernel.shape[0], TILE), F32),
            pltpu.VMEM((rows, 2 * TILE), LOW),
        ],
        flops=6 * rows * width * width,
    )


def project_back_kernel(
    kq0, dk0, dv0, far0, kq1, dk1, dv1, far1, qw0, kw0, vw0, qw1, kw1, vw1, x, gain, g,
    own, oth, gradient, low, sums, total,
):
    i = pl.program_id(0)
    count = pl.num_programs(0) // 2
    rows = x.shape[0]
    step = kq0.shape[1]
    at = pl.ds(pl.multiple_of(i * step, TILE), step)

    def part(kq, dk, dv, far, qw, kw, vw, target, start):
        kk = (dk[...] + far[0].astype(F32)).astype(LOW)
        kv = (dv[...] + far[1].astype(F32)).astype(LOW)
        target[0] = kk
        target[1] = kv
        product = dot_t(kq[...], qw[...]) + dot_t(kk, kw[...]) + dot_t(kv, vw[...])
        if start:
            total[...] = product
        else:
            total[...] += product
        ones = jnp.ones((8, rows), LOW)
        sums[16:24, at] = dot(ones, kq[...]) * 0.125
        sums[24:32, at] = dot(ones, kv) * 0.125

    first = (kq0, dk0, dv0, far0, qw0, kw0, vw0, own)
    pl.when(i == 0)(lambda: part(*first, True))
    pl.when((i > 0) & (i < count))(lambda: part(*first, False))
    pl.when(i >= count)(lambda: part(kq1, dk1, dv1, far1, qw1, kw1, vw1, oth, False))

    @pl.when(i == pl.num_programs(0) - 1)
    def _():
        def step(rows_at, carry):
            upstream = total[rows_at, :]
            change, hat = norm_back(upstream, x[rows_at, :], gain[...])
            value = g[rows_at, :] + change
            gradient[rows_at, :] = value
            low[rows_at, :] = (0.5 * value).astype(LOW)
            return carry[0] + fold(upstream * hat), carry[1] + fold(upstream)

        zero = jnp.zeros((8, x.shape[1]), F32)
        first, second = row_loop(rows, step, (zero, zero))
        sums[0:8, :] = first
        sums[8:16, :] = second


def project_back(own, oth, qw, kw, vw, x, gain, g):
    rows, width = x.shape
    half = width // 2
    tile = 256
    count = half // tile
    wide, thin = whole((rows, width)), whole((1, width))

    def flat(side):
        return pl.BlockSpec((rows, tile), lambda i: (0, side(i, count)))

    def stacked(side):
        return pl.BlockSpec((2, rows, tile), lambda i: (0, 0, side(i, count)))

    weight = lambda side: pl.BlockSpec((width, tile), lambda i: (0, side(i, count)))
    return launch(
        project_back_kernel,
        "project_back",
        (2 * count,),
        (*own, *oth, qw[0], kw[0], vw[0], qw[1], kw[1], vw[1], x, gain, g),
        [flat(first_half)] * 3
        + [stacked(first_half)]
        + [flat(second_half)] * 3
        + [stacked(second_half)]
        + [weight(first_half)] * 3
        + [weight(second_half)] * 3
        + [wide, thin, wide],
        [
            shape((2, rows, half), LOW),
            shape((2, rows, half), LOW),
            shape((rows, width), F32),
            shape((rows, width), LOW),
            shape((32, width), F32),
        ],
        [stacked(first_half), stacked(second_half), wide, wide, whole((32, width))],
        scratch=[pltpu.VMEM((rows, width), F32)],
        flops=6 * rows * width * width,
    )


def bit_order(devices, color):
    first = ((0, 1, 2), (1, 0, 2), (0, 1, 2), (1, 2, 0), (2, 0, 1))[color]
    return [*first, *range(3, devices.bit_length() - 1)]


def weight_kernel(devices, plan, sides, pairs, me, *refs):
    used = sorted({color for _, _, color in plan})
    places = sorted({(side, color) for side, _, color in plan})
    lefts, refs = refs[: 2 * sides], refs[2 * sides :]
    inputs, refs = refs[: 2 * pairs], refs[2 * pairs :]
    outs, turned = refs[: 2 * len(used)], refs[2 * len(used) :]
    rows, width = lefts[0].shape
    block = width // devices
    half = width // 2
    i = pl.program_id(0)

    def arrange(side):
        colors = [color for item, color in places if item == side]
        for part, source in enumerate(lefts[2 * side : 2 * side + 2]):
            for lane in range(0, width, TILE):
                piece = jnp.transpose(source[:, lane : lane + TILE].astype(F32)).astype(LOW)
                for inner in range(0, TILE, block):
                    relative = ((lane + inner) // block) ^ me[0]
                    for color in colors:
                        place = 0
                        for level, bit in enumerate(bit_order(devices, color)):
                            flag = 1 - ((relative >> bit) & 1)
                            place = place + flag * (devices >> (level + 1))
                        start = pl.multiple_of(place * block, block)
                        turned[places.index((side, color))][
                            pl.ds(start, block), part * rows : (part + 1) * rows
                        ] = piece[inner : inner + block, :]

    for step, (side, source, color) in enumerate(plan):
        fresh = side not in [item[0] for item in plan[:step]]

        def work(side=side, source=source, color=color, fresh=fresh):
            if fresh:
                arrange(side)
            q0, q1 = (ref if len(ref.shape) == 2 else ref.at[0] for ref in inputs[2 * source : 2 * source + 2])
            left = turned[places.index((side, color))]
            slot = used.index(color)
            product = dot(left[:, :rows], q0[...]) + dot(left[:, rows:], q1[...])
            outs[2 * slot][...] = product[:half].astype(LOW)
            outs[2 * slot + 1][...] = product[half:].astype(LOW)

        pl.when(i == step)(work)


def weight_gradient(devices, me, lefts, jobs, tile):
    rows, width = lefts[0][0].shape
    specs, operands, plan = [whole((rows, width))] * (2 * len(lefts)), [item for pair in lefts for item in pair], []
    for source, (side, pair, colors) in enumerate(jobs):
        first, last = len(plan), len(colors) - 1
        if pair[0].ndim == 2:
            spec = pl.BlockSpec((rows, tile), lambda i, *_, f=first, t=last: (0, jnp.clip(i - f, 0, t)))
        else:
            per = pair[0].shape[2] // tile

            def pick(i, *_, f=first, t=last, per=per):
                place = jnp.clip(i - f, 0, t)
                return place // per, 0, place % per

            spec = pl.BlockSpec((1, rows, tile), pick)
        specs += [spec, spec]
        operands += list(pair)
        plan += [(side, source, color) for color in colors]
    used = sorted({color for _, _, color in plan})
    outs, out_specs = [], []
    for color in used:
        steps = [step for step, item in enumerate(plan) if item[2] == color]

        def column(i, *_, steps=steps):
            place = 0
            for step in steps[1:]:
                place = place + jnp.where(i >= step, 1, 0)
            return 0, place

        outs += [shape((width // 2, tile * len(steps)), LOW)] * 2
        out_specs += [pl.BlockSpec((width // 2, tile), column)] * 2
    places = {(side, color) for side, _, color in plan}
    return launch(
        functools.partial(weight_kernel, devices, plan, len(lefts), len(jobs)),
        "weight_gradient",
        (len(plan),),
        operands,
        specs,
        outs,
        out_specs,
        scratch=[pltpu.VMEM((width, 2 * rows), LOW)] * len(places),
        scalars=(me,),
        flops=4 * rows * width * tile * len(plan),
    )


def gather_kernel(early, late, query_bias, value_bias, gain, shift, kernel, out):
    width = query_bias.shape[1]
    out[0:1, :] = early[...]
    out[1:2, :] = late[...]
    for slot, item in enumerate((query_bias, value_bias, gain, shift)):
        out[2 + slot : 3 + slot, :width] = item[...]
    out[8 : 8 + kernel.shape[0], :width] = kernel[...]


def gather(early, late, items, kernel):
    operands = (early, late, *items, kernel)
    rows = 8 + (kernel.shape[0] + 7) // 8 * 8
    return launch(
        gather_kernel,
        "gather",
        (1,),
        operands,
        [whole(item.shape) for item in operands],
        [shape((rows, early.shape[1]), F32)],
        [whole((rows, early.shape[1]))],
    )[0]


def swap(values):
    return lax.ppermute(values, "tensor", [(0, 1), (1, 0)])


def cross(values, devices, mask):
    return lax.ppermute(values, "dp", [(i, i ^ mask) for i in range(devices)])


def whole_slice(devices, block):
    return devices & (devices - 1) or devices < 8 or block % 16 or TILE % block


class Reduction:
    def __init__(self, devices, me, lefts, jobs, tile=512):
        self.devices = devices
        self.tile = tile
        self.colors = sorted({color for _, _, colors in jobs for color in colors})
        self.order = {color: [] for color in self.colors}
        for job, (_, pair, colors) in enumerate(jobs):
            for place, color in enumerate(colors):
                self.order[color].append((job, place))
        self.level = 0
        self.rows = lefts[0][0].shape[1]
        self.state = []
        self.result = None
        if whole_slice(devices, lefts[0][0].shape[1] // devices):
            pieces = []
            for side, pair, colors in jobs:
                both = jnp.concatenate([item if item.ndim == 2 else item[: -(-tile * len(colors) // item.shape[2])] for item in pair], axis=-2)
                if both.ndim == 3:
                    both = jnp.concatenate(list(both), axis=1)[:, : tile * len(colors)]
                left = jnp.concatenate(lefts[side], axis=0)
                pieces.append(dot(left, both, ((0,), (0,))).astype(LOW))
            total = lax.psum_scatter(jnp.concatenate(pieces, axis=1), "dp", scatter_dimension=0, tiled=True)
            cuts = [0]
            for piece in pieces:
                cuts.append(cuts[-1] + piece.shape[1])
            self.result = [total[:, a:b].astype(F32) for a, b in zip(cuts, cuts[1:])]
            return
        parts = weight_gradient(devices, me, lefts, jobs, tile)
        self.state = list(parts)

    def send(self):
        if self.result is not None:
            return
        for slot in range(len(self.state) // 2):
            bit = bit_order(self.devices, self.colors[slot])[self.level]
            self.state[2 * slot] = cross(self.state[2 * slot], self.devices, 1 << bit)

    def add(self):
        if self.result is not None:
            return
        self.level += 1
        arrived, kept = self.state[::2], self.state[1::2]
        half = kept[0].shape[0] // 2
        if half * 2 * self.devices == self.rows:
            self.state = [arrived[0].astype(F32) + kept[0].astype(F32)]
            return
        away = [one[:half] + two[:half] for one, two in zip(arrived, kept)]
        stay = [one[half:] + two[half:] for one, two in zip(arrived, kept)]
        bits = {bit_order(self.devices, color)[self.level] for color in self.colors}
        if len(bits) == 1 and len(away) > 1:
            away, stay = [jnp.concatenate(away, axis=1)], [jnp.concatenate(stay, axis=1)]
        self.state = [item for pair in zip(away, stay) for item in pair]

    def parts(self):
        if self.result is not None:
            return self.result
        tile = self.tile
        found = {}
        keys = [key for color in self.colors for key in self.order[color]]
        for column, key in enumerate(keys):
            found[key] = self.state[0][:, column * tile : (column + 1) * tile]
        jobs = sorted({job for job, _ in found})
        return [
            jnp.concatenate([found[key] for key in sorted(found) if key[0] == job], axis=1) for job in jobs
        ]


def hold(main, *reductions):
    flat = list(main)
    for item in reductions:
        flat += item.state
    flat = lax.optimization_barrier(tuple(flat))
    place = len(main)
    for item in reductions:
        count = len(item.state)
        item.state = list(flat[place : place + count])
        place += count
    return flat[: len(main)]


def pack_kernel(late, final, mixer, attended, depth, early, dkernel, dtable0, dtable1, t10, t11, t40, t41, own, oth, table):
    width = late.shape[1]
    half = width // 2
    own[...] = jnp.zeros_like(own)
    oth[...] = jnp.zeros_like(oth)
    rolled = dtable0[...] + dtable1[...]
    table[0:REL, :] = rolled[0:REL]
    table[REL - 1 : REL, :] = jnp.sum(rolled[REL - 1 :], axis=0, keepdims=True)
    table[REL:, :] = jnp.zeros((table.shape[0] - REL, TILE), F32)

    def folded(source, group):
        return jnp.sum(source[8 * group : 8 * group + 8, :], axis=0, keepdims=True)

    shared = [folded(late, g) for g in range(3)] + [folded(final, g) for g in range(2)]
    shared += [folded(mixer, g) for g in range(3)] + [folded(attended, g) for g in range(2)]
    shared += [folded(early, g) for g in range(3)]
    mixed = [folded(attended, g) for g in (2, 3)] + [folded(depth, g) for g in range(2)]
    for target, start, tallies in ((own, 0, (t10, t40)), (oth, half, (t11, t41))):
        for place, item in enumerate(shared):
            target[place : place + 1, :] = item
        for g in range(8):
            target[SHARED - 11 : SHARED - 1, g * TILE : (g + 1) * TILE] = table[10 * g : 10 * g + 10, :]
        for place, item in enumerate(mixed):
            target[SHARED + place : SHARED + place + 1, :half] = item[:, start : start + half]
        target[SHARED + 4 : SHARED + 18, :half] = dkernel[0:14, start : start + half]
        target[SHARED : SHARED + 17, half:] = dkernel[14:31, start : start + half]
        place = SHARED + 18
        for item in tallies:
            for begin in range(0, item.shape[1], width):
                target[place : place + 1, :] = item[0:1, begin : begin + width]
                place += 1


def pack(operands):
    width = operands[0].shape[1]
    rows = SHARED + 24
    return launch(
        pack_kernel,
        "pack",
        (1,),
        operands,
        [whole(item.shape) for item in operands],
        [shape((rows, width), F32)] * 2,
        [whole((rows, width))] * 2,
        scratch=[pltpu.VMEM((80, TILE), F32)],
    )


def shards(
    devices,
    inputs,
    cotangent,
    slot_flags,
    early_norm_gain,
    early_norm_shift,
    early_up,
    early_up_bias,
    early_down,
    early_down_bias,
    attend_norm_gain,
    attend_norm_shift,
    query_weight,
    query_bias,
    key_weight,
    value_weight,
    value_bias,
    distance_table,
    attend_weight,
    attend_bias,
    mixer_norm_gain,
    mixer_norm_shift,
    gated_weight,
    depth_kernel,
    depth_norm_gain,
    depth_norm_shift,
    mixer_weight,
    late_norm_gain,
    late_norm_shift,
    late_up,
    late_up_bias,
    late_down,
    late_down_bias,
    final_gain,
    final_shift,
):
    row = lambda vector: vector[None, :]
    both = lambda weight: (weight, swap(weight))
    side = lax.axis_index("tensor").astype(jnp.int32)
    core = side[None]
    me = lax.axis_index("dp").astype(jnp.int32)[None]
    half = depth_kernel.shape[1]
    hidden = early_up.shape[1]
    taps = depth_kernel.shape[0]

    vectors = (query_bias, value_bias, depth_norm_gain, depth_norm_shift)
    small = gather(row(early_up_bias), row(late_up_bias), [row(item) for item in vectors], depth_kernel)
    other = swap(small)
    early_bias = (row(early_up_bias), other[0:1])
    late_bias = (row(late_up_bias), other[1:2])
    query_bias_all, value_bias_all, depth_gain_all, depth_shift_all = [
        jnp.concatenate([row(item), other[2 + slot : 3 + slot, :half]], axis=1)
        for slot, item in enumerate(vectors)
    ]
    kernel_all = jnp.concatenate([small[8 : 9 + taps, :half], other[8 : 9 + taps, :half]], axis=1)
    early_up_all, early_down_all = both(early_up), both(early_down)
    key_all, value_all, query_all = both(key_weight), both(value_weight), both(query_weight)
    table = distance_table.astype(LOW)
    table = jnp.concatenate([table, jnp.broadcast_to(table[REL - 1 :], (TILE - REL, HEAD_DIM))], axis=0)
    table = jnp.concatenate([table, table], axis=1)

    n1, s10, a10, x1 = feed_half(
        True, inputs, (row(early_norm_gain), row(early_norm_shift)), early_up_all[0], early_bias[0], early_down_all[0]
    )
    s11, a11, x1 = feed_half(
        False, inputs, (n1, x1, row(early_down_bias)), early_up_all[1], early_bias[1], early_down_all[1]
    )
    n2, kv = project(x1, row(attend_norm_gain), row(attend_norm_shift), key_all, value_all, value_bias_all)
    kvr = swap(kv)
    q = query(n2, query_all, query_bias_all)
    attend_all, gated_all = both(attend_weight), both(gated_weight)
    q, attend_other, gated_other = hold((q, attend_all[1], gated_all[1]))
    attend_all, gated_all = (attend_weight, attend_other), (gated_weight, gated_other)
    o, lse = attend(core, q, kv, kvr, table)
    o, late_up, late_down, mixer_weight = hold((o, late_up, late_down, mixer_weight))
    mixer_all = both(mixer_weight)
    late_up_all, late_down_all = both(late_up), both(late_down)
    n1p, a1p, n2p = swap(n1), swap(a11), swap(n2)
    x2, n3, u, sig, edge = mixer_in(
        o, x1, attend_all, row(attend_bias), row(mixer_norm_gain), row(mixer_norm_shift), gated_all
    )
    edge = lax.ppermute(edge, "tensor", [(0, 1)])
    op, n3p = swap(o[1:]), swap(n3)
    z, w0, w1, x3 = mixer_out(u, edge, kernel_all, depth_gain_all, depth_shift_all, mixer_all, x2)
    wp = swap(w1)
    x3, n1p, a1p, n2p = hold((x3, n1p, a1p, n2p))
    n4, s40, s41, a40, a41, x4 = feed_forward(
        x3, row(late_norm_gain), row(late_norm_shift), late_up_all, late_bias, late_down_all, row(late_down_bias)
    )
    n4p, a4p = swap(n4), swap(a41)
    x4, op, n3p, wp = hold((x4, op, n3p, wp))
    output, g4, d4, final_sums = final_norm(slot_flags, x4, cotangent, row(final_gain), row(final_shift))
    d4p = swap(d4)

    reduction = functools.partial(Reduction, devices, me)
    k40, k41, t40, t41, g3, d3, late_sums = feed_back(
        1.0, g4, d4, x3, row(late_norm_gain), late_up_all, late_down_all, (s40, s41)
    )
    d3, d4p, n4p, a4p = hold((d3, d4p, n4p, a4p))
    k4p, d3p = swap(k41), swap(d3)
    one = reduction([(d4, d4p)], [(0, (a40, a4p), (0, 0, 1, 1))])
    (d3,) = hold((d3,), one)
    one.send()
    bz, depth_sums, head = mixer_mid(d3, mixer_all, z, depth_gain_all, depth_shift_all)
    tail = lax.ppermute(head, "tensor", [(1, 0)])
    k4p, d3p, bz = hold((k4p, d3p, bz))
    two = reduction([(n4, n4p)], [(0, (k40, k4p), (0, 0, 1, 1))])
    (bz,) = hold((bz,), two)
    two.send()
    ka0, ka1, dkernel, g2, d2, do0, do1, mixer_sums = mixer_back(
        bz, tail, u, edge, kernel_all, sig, gated_all, x2, row(mixer_norm_gain), g3, attend_all
    )
    kap, d2p = swap(ka1), swap(d2)
    one.add()
    do0, kap, d2p = hold((do0, kap, d2p), one)
    one.send()
    kq0, dk0, dv0, dkv0, dtable0 = attend_back(core, 0, q, do0, o, kv, kvr, table, lse)
    far1 = swap(dkv0)
    one.add()
    two.add()
    three = reduction(
        [(d3, d3p), (n3, n3p), (d2, d2p)],
        [(0, (w0, wp), (0,)), (1, (ka0, kap), (0, 1)), (2, (o, op), (1,))],
    )
    do1, kq0, far1 = hold((do1, kq0, far1), one, two, three)
    one.send()
    two.send()
    three.send()
    kq1, dk1, dv1, dkv1, dtable1 = attend_back(core, q.shape[1] // TILE // 2, q, do1, o, kv, kvr, table, lse)
    far0, kqp = swap(dkv1), swap(kq1)
    one.add()
    two.add()
    three.add()
    dk0, kq1 = hold((dk0, kq1), one, two, three)
    one.send()
    two.send()
    three.send()
    kk0, kk1, g1, d1, attend_sums = project_back(
        (kq0, dk0, dv0, far0), (kq1, dk1, dv1, far1), query_all, key_all, value_all, x1, row(attend_norm_gain), g2
    )
    d1p, kkp = swap(d1), swap(kk1)
    one.add()
    two.add()
    three.add()
    d1p, kkp = hold((d1p, kkp), one, two, three)
    two.send()
    three.send()
    four = reduction(
        [(d1, d1p), (n2, n2p)],
        [
            (0, (a10, a1p), (2, 2, 2, 3, 3, 3, 4, 4)),
            (1, (kq0, kqp), (2, 2)),
            (1, (kk0, kkp), (3, 3, 4, 4)),
        ],
        256,
    )
    (d1,) = hold((d1,), four)
    four.send()
    k10, k11, t10, t11 = feed_key(d1, early_down_all, (s10, s11))
    k1p = swap(k11)
    two.add()
    three.add()
    (k10,) = hold((k10,), two, three)
    three.send()
    gradient, early_sums = feed_end(g1, d1, inputs, row(early_norm_gain), early_up_all, (k10, k11))
    three.add()
    (early_sums,) = hold((early_sums,), four)
    four.add()
    early_sums, k1p = hold((early_sums, k1p), four, three)
    four.send()
    small_own, small_oth = pack(
        (
            late_sums, final_sums, mixer_sums, attend_sums, depth_sums, early_sums, dkernel,
            dtable0, dtable1, t10, t11, t40, t41,
        )
    )
    first = small_own
    masks = [1 << bit for bit in (3, 0, 1, 2, *range(4, devices.bit_length() - 1))]
    if devices & (devices - 1) or devices < 16:
        masks = []
    n1, small_oth = hold((n1, small_oth))
    moved = swap(small_oth)
    five = reduction([(n1, n1p)], [(0, (k10, k1p), (2, 2, 2, 3, 3, 3, 4, 4))], 256)
    first, moved = hold((first, moved), five)
    five.send()
    for step in range(4):
        first = first + moved
        moved = cross(first, devices, masks[step]) if masks else jnp.zeros_like(first)
        if step < 3:
            four.add()
        if step < 2:
            four.send()
        five.add()
        (first,) = hold((first,), four, five)
        if step < 3:
            five.send()
    first = first + moved
    for mask in masks[4:]:
        first = first + cross(first, devices, mask)
    if not masks:
        first = lax.psum(first, "dp")
    (late_down_sum,) = one.parts()
    (late_up_sum,) = two.parts()
    mixer_sum, gated_sum, attend_sum = three.parts()
    early_down_sum, query_sum, project_sum = four.parts()
    (early_up_sum,) = five.parts()

    table_out = jnp.concatenate(
        [first[SHARED - 11 : SHARED - 1, g * TILE : (g + 1) * TILE] for g in range(8)], axis=0
    )[:REL]
    table_out = table_out[:, :HEAD_DIM] + table_out[:, HEAD_DIM:]
    left, right = first[SHARED : SHARED + 18, :half], first[SHARED : SHARED + 17, half:]
    pile_sum = jnp.concatenate([left, right], axis=0)
    early_rows = first[10:13]
    count = hidden // (2 * half)
    early_up_bias_sum = first[SHARED + 18 : SHARED + 18 + count].reshape(-1)
    late_up_bias_sum = first[SHARED + 18 + count : SHARED + 18 + 2 * count].reshape(-1)
    return (
        output,
        gradient,
        early_rows[0],
        early_rows[1],
        early_up_sum,
        early_up_bias_sum,
        early_down_sum.T,
        early_rows[2],
        first[8],
        first[9],
        query_sum,
        pile_sum[0],
        project_sum[:, :half],
        project_sum[:, half:],
        pile_sum[1],
        table_out,
        attend_sum.T,
        first[7],
        first[5],
        first[6],
        jnp.stack([gated_sum[:, :half], gated_sum[:, half:]]),
        pile_sum[4:],
        pile_sum[2],
        pile_sum[3],
        mixer_sum.T,
        first[0],
        first[1],
        late_up_sum,
        late_up_bias_sum,
        late_down_sum.T,
        first[2],
        first[3],
        first[4],
    )


def solution(mesh):
    placed = (
        P(("dp", "tensor"), None),
        P(("dp", "tensor"), None),
        P("dp"),
        P(),
        P(),
        P(None, "tensor"),
        P("tensor"),
        P("tensor", None),
        P(),
        P(),
        P(),
        P(None, "tensor"),
        P("tensor"),
        P(None, "tensor"),
        P(None, "tensor"),
        P("tensor"),
        P(),
        P("tensor", None),
        P(),
        P(),
        P(),
        P(None, None, "tensor"),
        P(None, "tensor"),
        P("tensor"),
        P("tensor"),
        P("tensor", None),
        P(),
        P(),
        P(None, "tensor"),
        P("tensor"),
        P("tensor", None),
        P(),
        P(),
        P(),
    )
    return jax.shard_map(
        functools.partial(shards, mesh.shape["dp"]),
        mesh=mesh,
        in_specs=placed,
        out_specs=(
            P(("dp", "tensor"), None),
            P(("dp", "tensor"), None),
            P(),
            P(),
            P("dp", "tensor"),
            P("tensor"),
            P("tensor", "dp"),
            P(),
            P(),
            P(),
            P("dp", "tensor"),
            P("tensor"),
            P("dp", "tensor"),
            P("dp", "tensor"),
            P("tensor"),
            P(),
            P("tensor", "dp"),
            P(),
            P(),
            P(),
            P(None, "dp", "tensor"),
            P(None, "tensor"),
            P("tensor"),
            P("tensor"),
            P("tensor", "dp"),
            P(),
            P(),
            P("dp", "tensor"),
            P("tensor"),
            P("tensor", "dp"),
            P(),
            P(),
            P(),
        ),
        check_vma=False,
    )
```

```python
import functools

import jax
import jax.numpy as jnp
from jax import lax
from jax.experimental import pallas as pl
from jax.experimental.pallas import tpu as pltpu
from jax.sharding import PartitionSpec as P

HEAD_DIM = 64
LEFT = 64
RIGHT = 8
REL = LEFT + RIGHT + 1
TILE = 128
HALO = 32
CHUNK = 64
GRANT = 58 << 20
EPS = 1e-05
SHARED = 24
LOW = jnp.bfloat16
F32 = jnp.float32


def dot(left, right, dims=((1,), (0,))):
    return lax.dot_general(left, right, (dims, ((), ())), preferred_element_type=F32)


def dot_t(left, right):
    return dot(left, right, ((1,), (1,)))


def sigmoid(values):
    return 0.5 * jnp.tanh(0.5 * values) + 0.5


def shape(dims, kind):
    return jax.ShapeDtypeStruct(dims, kind)


def whole(dims):
    return pl.BlockSpec(dims, lambda i, *_: (0,) * len(dims))


def first_half(i, count):
    return jnp.minimum(i, count - 1)


def second_half(i, count):
    return jnp.maximum(i - count, 0)


def launch(body, name, grid, operands, specs, outs, out_specs, scratch=(), scalars=(), flops=0):
    moved = sum(item.size * item.dtype.itemsize for item in (*operands, *outs))
    return pl.pallas_call(
        body,
        grid_spec=pltpu.PrefetchScalarGridSpec(
            num_scalar_prefetch=len(scalars),
            grid=grid,
            in_specs=specs,
            out_specs=out_specs,
            scratch_shapes=list(scratch),
        ),
        out_shape=outs,
        compiler_params=pltpu.CompilerParams(
            dimension_semantics=("arbitrary",) * len(grid), vmem_limit_bytes=GRANT
        ),
        cost_estimate=pl.CostEstimate(flops=flops, transcendentals=0, bytes_accessed=moved),
        name=name,
    )(*scalars, *operands)


def normed_rows(values):
    center = values - jnp.mean(values, axis=1, keepdims=True)
    inverse = lax.rsqrt(jnp.mean(center * center, axis=1, keepdims=True) + EPS)
    return center * inverse, inverse


def row_loop(rows, body, initial=0):
    def step(i, carry):
        return body(pl.ds(pl.multiple_of(i * CHUNK, CHUNK), CHUNK), carry)

    return lax.fori_loop(0, rows // CHUNK, step, initial)


def norm_into(source, gain, shift, target):
    def rows(at, carry):
        hat, _ = normed_rows(source[at, :].astype(F32))
        target[at, :] = (hat * gain[...] + shift[...]).astype(LOW)
        return carry

    row_loop(source.shape[0], rows)


def fold(values):
    return jnp.sum(values.reshape(values.shape[0] // 8, 8, values.shape[1]), axis=0)


def norm_back(upstream, values, gain):
    hat, inverse = normed_rows(values)
    scaled = upstream * gain
    first = jnp.mean(scaled, axis=1, keepdims=True)
    second = jnp.mean(scaled * hat, axis=1, keepdims=True)
    return inverse * (scaled - first - hat * second), hat


def feed_kernel(x, gain, shift, up0, up1, bias0, bias1, down0, down1, bias, n, s0, s1, a0, a1, out):
    i = pl.program_id(0)
    count = pl.num_programs(0) // 2

    @pl.when(i == 0)
    def _():
        norm_into(x, gain, shift, n)

    def part(up, up_bias, down, slope, active, start):
        hidden = dot(n[...], up[...]) + up_bias[...]
        gate = sigmoid(hidden)
        swished = hidden * gate
        slope[...] = (gate + swished * (1.0 - gate)).astype(LOW)
        low = swished.astype(LOW)
        active[...] = low
        product = dot(low, down[...])
        if start:
            out[...] = product
        else:
            out[...] += product

    pl.when(i == 0)(lambda: part(up0, bias0, down0, s0, a0, True))
    pl.when((i > 0) & (i < count))(lambda: part(up0, bias0, down0, s0, a0, False))
    pl.when(i >= count)(lambda: part(up1, bias1, down1, s1, a1, False))

    @pl.when(i == 2 * count - 1)
    def _():
        def rows(at, carry):
            out[at, :] = x[at, :].astype(F32) + 0.5 * (out[at, :] + bias[...])
            return carry

        row_loop(x.shape[0], rows)


def feed_forward(x, gain, shift, up, up_bias, down, bias):
    rows, width = x.shape
    hidden = up[0].shape[1]
    tile = min(512, hidden)
    count = hidden // tile
    own = functools.partial(first_half, count=count)
    oth = functools.partial(second_half, count=count)
    column = lambda height, pick: pl.BlockSpec((height, tile), lambda i: (0, pick(i)))
    row = lambda pick: pl.BlockSpec((tile, width), lambda i: (pick(i), 0))
    return launch(
        feed_kernel,
        "feed_forward",
        (2 * count,),
        (x, gain, shift, *up, *up_bias, *down, bias),
        [
            whole((rows, width)),
            whole((1, width)),
            whole((1, width)),
            column(width, own),
            column(width, oth),
            column(1, own),
            column(1, oth),
            row(own),
            row(oth),
            whole((1, width)),
        ],
        [shape((rows, width), LOW)] + [shape((rows, hidden), LOW)] * 4 + [shape((rows, width), F32)],
        [
            whole((rows, width)),
            column(rows, own),
            column(rows, oth),
            column(rows, own),
            column(rows, oth),
            whole((rows, width)),
        ],
        flops=8 * rows * width * hidden,
    )


def feed_half_kernel(first, x, *refs):
    i = pl.program_id(0)
    if first:
        gain, shift, up, up_bias, down, n, slope, active, out = refs
        pl.when(i == 0)(lambda: norm_into(x, gain, shift, n))
    else:
        n, prior, bias, up, up_bias, down, slope, active, out = refs
    hidden = dot(n[...], up[...]) + up_bias[...]
    gate = sigmoid(hidden)
    swished = hidden * gate
    slope[...] = (gate + swished * (1.0 - gate)).astype(LOW)
    low = swished.astype(LOW)
    active[...] = low
    product = dot(low, down[...])

    @pl.when(i == 0)
    def _():
        out[...] = product if first else prior[...] + product

    @pl.when(i > 0)
    def _():
        out[...] += product

    if not first:
        @pl.when(i == pl.num_programs(0) - 1)
        def _():
            def rows(at, carry):
                out[at, :] = x[at, :].astype(F32) + 0.5 * (out[at, :] + bias[...])
                return carry

            row_loop(x.shape[0], rows)


def feed_half(first, x, extra, up, up_bias, down):
    rows, width = x.shape
    hidden = up.shape[1]
    tile = min(512, hidden)
    column = lambda height: pl.BlockSpec((height, tile), lambda i: (0, i))
    outs = [shape((rows, width), LOW)] * first
    outs += [shape((rows, hidden), LOW)] * 2 + [shape((rows, width), F32)]
    return launch(
        functools.partial(feed_half_kernel, first),
        "feed_half",
        (hidden // tile,),
        (x, *extra, up, up_bias, down),
        [whole(item.shape) for item in (x, *extra)]
        + [column(width), column(1), pl.BlockSpec((tile, width), lambda i: (i, 0))],
        outs,
        [whole((rows, width))] * first + [column(rows), column(rows), whole((rows, width))],
        flops=4 * rows * width * hidden,
    )


def feed_back_kernel(scale, g, d, x, gain, up0, up1, down0, down1, s0, s1, k0, k1, t0, t1, out, *rest):
    i = pl.program_id(0)
    count = pl.num_programs(0) // 2
    low, sums, total = rest if scale else (None, *rest)

    def part(up, down, slope, key, tally, start):
        back = dot_t(d[...], down[...]) * slope[...].astype(F32)
        key_low = back.astype(LOW)
        key[...] = key_low
        tally[...] = dot(jnp.ones((8, key_low.shape[0]), LOW), key_low)
        product = dot_t(key_low, up[...])
        if start:
            total[...] = product
        else:
            total[...] += product

    pl.when(i == 0)(lambda: part(up0, down0, s0, k0, t0, True))
    pl.when((i > 0) & (i < count))(lambda: part(up0, down0, s0, k0, t0, False))
    pl.when(i >= count)(lambda: part(up1, down1, s1, k1, t1, False))

    @pl.when(i == 2 * count - 1)
    def _():
        def rows(at, carry):
            upstream = total[at, :]
            change, hat = norm_back(upstream, x[at, :].astype(F32), gain[...])
            gradient = g[at, :] + change
            out[at, :] = gradient
            if scale:
                low[at, :] = (scale * gradient).astype(LOW)
            return (
                carry[0] + fold(upstream * hat),
                carry[1] + fold(upstream),
                carry[2] + fold(d[at, :].astype(F32)),
            )

        zero = jnp.zeros((8, x.shape[1]), F32)
        first, second, third = row_loop(x.shape[0], rows, (zero, zero, zero))
        sums[0:8, :] = first
        sums[8:16, :] = second
        sums[16:24, :] = third


def feed_back(scale, g, d, x, gain, up, down, slope):
    rows, width = x.shape
    hidden = up[0].shape[1]
    tile = min(512, hidden)
    count = hidden // tile
    own = functools.partial(first_half, count=count)
    oth = functools.partial(second_half, count=count)
    column = lambda height, pick: pl.BlockSpec((height, tile), lambda i: (0, pick(i)))
    row = lambda pick: pl.BlockSpec((tile, width), lambda i: (pick(i), 0))
    outs = [shape((rows, hidden), LOW)] * 2 + [shape((8, hidden), F32)] * 2
    outs += [shape((rows, width), F32)] + [shape((rows, width), LOW)] * bool(scale)
    outs += [shape((24, width), F32)]
    return launch(
        functools.partial(feed_back_kernel, scale),
        "feed_back",
        (2 * count,),
        (g, d, x, gain, *up, *down, *slope),
        [
            whole((rows, width)),
            whole((rows, width)),
            whole((rows, width)),
            whole((1, width)),
            column(width, own),
            column(width, oth),
            row(own),
            row(oth),
            column(rows, own),
            column(rows, oth),
        ],
        outs,
        [column(rows, own), column(rows, oth), column(8, own), column(8, oth)]
        + [whole((rows, width))] * (1 + bool(scale))
        + [whole((24, width))],
        scratch=[pltpu.VMEM((rows, width), F32)],
        flops=8 * rows * width * hidden,
    )


def feed_key_kernel(d, down0, down1, s0, s1, k0, k1, t0, t1):
    i = pl.program_id(0)
    count = pl.num_programs(0) // 2

    def part(down, slope, key, tally):
        low = (dot_t(d[...], down[...]) * slope[...].astype(F32)).astype(LOW)
        key[...] = low
        tally[...] = dot(jnp.ones((8, low.shape[0]), LOW), low)

    pl.when(i < count)(lambda: part(down0, s0, k0, t0))
    pl.when(i >= count)(lambda: part(down1, s1, k1, t1))


def feed_key(d, down, slope):
    rows, width = d.shape
    hidden = slope[0].shape[1]
    tile = min(512, hidden)
    count = hidden // tile
    own = functools.partial(first_half, count=count)
    oth = functools.partial(second_half, count=count)
    column = lambda height, pick: pl.BlockSpec((height, tile), lambda i: (0, pick(i)))
    row = lambda pick: pl.BlockSpec((tile, width), lambda i: (pick(i), 0))
    return launch(
        feed_key_kernel,
        "feed_key",
        (2 * count,),
        (d, *down, *slope),
        [whole((rows, width)), row(own), row(oth), column(rows, own), column(rows, oth)],
        [shape((rows, hidden), LOW)] * 2 + [shape((8, hidden), F32)] * 2,
        [column(rows, own), column(rows, oth), column(8, own), column(8, oth)],
        flops=4 * rows * width * hidden,
    )


def feed_end_kernel(g, d, x, gain, up0, up1, k0, k1, out, sums, total):
    i = pl.program_id(0)
    count = pl.num_programs(0) // 2

    def part(up, key, start):
        product = dot_t(key[...], up[...])
        if start:
            total[...] = product
        else:
            total[...] += product

    pl.when(i == 0)(lambda: part(up0, k0, True))
    pl.when((i > 0) & (i < count))(lambda: part(up0, k0, False))
    pl.when(i >= count)(lambda: part(up1, k1, False))

    @pl.when(i == 2 * count - 1)
    def _():
        def rows(at, carry):
            upstream = total[at, :]
            change, hat = norm_back(upstream, x[at, :].astype(F32), gain[...])
            out[at, :] = g[at, :] + change
            return (
                carry[0] + fold(upstream * hat),
                carry[1] + fold(upstream),
                carry[2] + fold(d[at, :].astype(F32)),
            )

        zero = jnp.zeros((8, x.shape[1]), F32)
        first, second, third = row_loop(x.shape[0], rows, (zero, zero, zero))
        sums[0:8, :] = first
        sums[8:16, :] = second
        sums[16:24, :] = third


def feed_end(g, d, x, gain, up, key):
    rows, width = x.shape
    hidden = key[0].shape[1]
    tile = min(512, hidden)
    count = hidden // tile
    own = functools.partial(first_half, count=count)
    oth = functools.partial(second_half, count=count)
    column = lambda height, pick: pl.BlockSpec((height, tile), lambda i: (0, pick(i)))
    wide = whole((rows, width))
    return launch(
        feed_end_kernel,
        "feed_end",
        (2 * count,),
        (g, d, x, gain, *up, *key),
        [wide, wide, wide, whole((1, width))]
        + [column(width, own), column(width, oth), column(rows, own), column(rows, oth)],
        [shape((rows, width), F32), shape((24, width), F32)],
        [wide, whole((24, width))],
        scratch=[pltpu.VMEM((rows, width), F32)],
        flops=4 * rows * width * hidden,
    )


def final_kernel(flag, x, cotangent, gain, shift, out, gradient, low, sums):
    live = flag[0].astype(F32)

    @pl.when(pl.program_id(0) == 0)
    def _():
        sums[...] = jnp.zeros_like(sums)

    hat, inverse = normed_rows(x[...])
    out[...] = (live * (hat * gain[...] + shift[...])).astype(LOW)
    upstream = live * cotangent[...].astype(F32)
    scaled = upstream * gain[...]
    first = jnp.mean(scaled, axis=1, keepdims=True)
    second = jnp.mean(scaled * hat, axis=1, keepdims=True)
    change = inverse * (scaled - first - hat * second)
    gradient[...] = change
    low[...] = (0.5 * change).astype(LOW)
    sums[0:8, :] += fold(upstream * hat)
    sums[8:16, :] += fold(upstream)


def final_norm(flag, x, cotangent, gain, shift):
    rows, width = x.shape
    step = min(128, rows)
    block = pl.BlockSpec((step, width), lambda i, *_: (i, 0))
    return launch(
        final_kernel,
        "final_norm",
        (rows // step,),
        (x, cotangent, gain, shift),
        [block, block, whole((1, width)), whole((1, width))],
        [shape((rows, width), LOW), shape((rows, width), F32), shape((rows, width), LOW), shape((16, width), F32)],
        [block, block, block, whole((16, width))],
        scalars=(flag,),
    )


def project_kernel(x, gain, shift, kw0, kw1, vw0, vw1, vb, n, kv):
    i = pl.program_id(0)
    step = kw0.shape[1]
    width = x.shape[1]
    half = width // 2

    @pl.when(i == 0)
    def _():
        norm_into(x, gain, shift, n)

    for side, (kw, vw) in enumerate(((kw0, vw0), (kw1, vw1))):
        at = pl.ds(pl.multiple_of(side * half + i * step, step), step)
        to = pl.ds(pl.multiple_of(width + side * half + i * step, step), step)
        kv[:, at] = dot(n[...], kw[...]).astype(LOW)
        kv[:, to] = (dot(n[...], vw[...]) + vb[:, at]).astype(LOW)


def project(x, gain, shift, kw, vw, vb):
    rows, width = x.shape
    half = width // 2
    step = 256
    weight = pl.BlockSpec((width, step), lambda i: (0, i))
    thin = whole((1, width))
    return launch(
        project_kernel,
        "project",
        (half // step,),
        (x, gain, shift, *kw, *vw, vb),
        [whole((rows, width)), thin, thin] + [weight] * 4 + [thin],
        [shape((rows, width), LOW), shape((rows, 2 * width), LOW)],
        [whole((rows, width)), whole((rows, 2 * width))],
        flops=4 * rows * width * width,
    )


def query_kernel(n, qw0, qw1, qb, q):
    i = pl.program_id(0)
    step = qw0.shape[1]
    half = q.shape[1] // 2
    for side, qw in enumerate((qw0, qw1)):
        at = pl.ds(pl.multiple_of(side * half + i * step, step), step)
        q[:, at] = ((dot(n[...], qw[...]) + qb[:, at]).astype(LOW).astype(F32) * HEAD_DIM**-0.5).astype(LOW)


def query(n, qw, qb):
    rows, width = n.shape
    half = width // 2
    step = 256
    weight = pl.BlockSpec((width, step), lambda i: (0, i))
    wide = whole((rows, width))
    return launch(
        query_kernel,
        "query",
        (half // step,),
        (n, *qw, qb),
        [wide, weight, weight, whole((1, width))],
        [shape((rows, width), LOW)],
        [wide],
        flops=2 * rows * width * width,
    )[0]


def in_head(head, dims):
    return (lax.broadcasted_iota(jnp.int32, dims, 1) // HEAD_DIM) == head


def band_of(block):
    rows = block.shape[0]
    left = jnp.broadcast_to(block[:, 0:1], (rows, TILE))
    right = jnp.broadcast_to(block[:, TILE - 1 : TILE], (rows, TILE))
    lane = lax.broadcasted_iota(jnp.int32, (rows, TILE), 1)
    mixed = jnp.where(lane < TILE // 2, right, left)
    spread = jnp.concatenate([block, right, mixed, left], axis=1)
    band = pltpu.roll(spread, LEFT, 1, stride=1, stride_axis=0)
    return left, right, [band[:, t * TILE : (t + 1) * TILE] for t in range(3)]


def attend_kernel(core, q, k0, v0, k1, v1, table, o, lse, prob, scores):
    rows = q.shape[0]
    blocks = rows // TILE
    second = core[0] == 1
    mixed = []
    peaks = []
    for head in range(2):
        inside = in_head(head, q.shape)
        query = jnp.where(inside, q[...], jnp.zeros_like(q))
        scores[:, :rows] = dot_t(query, k0[...])
        scores[:, rows:] = dot_t(query, k1[...])
        relative = dot_t(query, table[...])
        totals = []
        for b in range(blocks):
            at = slice(b * TILE, (b + 1) * TILE)
            left, right, band = band_of(relative[at, :])
            far = jnp.where(second, left, right)
            tiles = []
            for t in range(blocks):
                gap = t - b
                term = left if gap <= -2 else right if gap >= 2 else band[gap + 1]
                tiles.append(scores[at, t * TILE : (t + 1) * TILE] + term)
            for t in range(blocks):
                term = far
                if b == blocks - 1 and t == 0:
                    term = jnp.where(second, left, band[2])
                if b == 0 and t == blocks - 1:
                    term = jnp.where(second, band[0], right)
                tiles.append(scores[at, rows + t * TILE : rows + (t + 1) * TILE] + term)
            peak = functools.reduce(jnp.maximum, tiles)
            peak = jnp.max(peak, axis=1, keepdims=True)
            total = jnp.zeros((TILE, TILE), F32)
            for t, tile in enumerate(tiles):
                value = jnp.exp(tile - peak)
                total = total + value
                prob[at, t * TILE : (t + 1) * TILE] = value.astype(LOW)
            total = jnp.sum(total, axis=1, keepdims=True)
            totals.append((peak, total))
        product = dot(prob[:, :rows], v0[...]) + dot(prob[:, rows:], v1[...])
        mixed.append(
            jnp.concatenate(
                [
                    product[b * TILE : (b + 1) * TILE] * (1.0 / totals[b][1])
                    for b in range(blocks)
                ],
                axis=0,
            )
        )
        peaks.append(jnp.concatenate([peak + jnp.log(total) for peak, total in totals], axis=0))
    o[0] = jnp.where(in_head(0, q.shape), mixed[0], mixed[1]).astype(LOW)
    lane = lax.broadcasted_iota(jnp.int32, (rows, TILE), 1)
    columns = jnp.where(lane == 0, peaks[0], jnp.where(lane == 1, peaks[1], 0.0))
    lse[...] = jnp.transpose(columns)[0:8, :]


def pair_specs(rows, pairs, start):
    near = pl.BlockSpec((rows, TILE), lambda i, *_: (0, start + i))
    near_value = pl.BlockSpec((rows, TILE), lambda i, *_: (0, pairs + start + i))
    far = pl.BlockSpec((rows, TILE), lambda i, *_: (0, (start + i + pairs // 2) % pairs))
    far_value = pl.BlockSpec((rows, TILE), lambda i, *_: (0, pairs + (start + i + pairs // 2) % pairs))
    return [near, near_value, far, far_value]


def attend(core, q, kv, kvr, table):
    rows, width = q.shape
    pairs = width // TILE
    specs = pair_specs(rows, pairs, 0)
    count = pairs // 2
    joined = pl.BlockSpec((1, rows, TILE), lambda i, *_: (i // count, 0, i % count))
    return launch(
        attend_kernel,
        "attend",
        (pairs,),
        (q, kv, kv, kvr, kvr, table),
        [specs[0], *specs, whole((TILE, TILE))],
        [shape((2, rows, width // 2), LOW), shape((8 * pairs, rows), F32)],
        [joined, pl.BlockSpec((8, rows), lambda i, *_: (i, 0))],
        scratch=[pltpu.VMEM((rows, 2 * rows), LOW), pltpu.VMEM((rows, 2 * rows), F32)],
        scalars=(core,),
        flops=8 * rows * rows * width,
    )


def attend_back_kernel(
    core, q, do, o, k0, v0, k1, v1, table, lse, kq, dk0, dv0, dkv1, dtable, prob, slope, scores, ds_back, de
):
    rows = q.shape[0]
    blocks = rows // TILE
    second = core[0] == 1

    @pl.when(pl.program_id(0) == 0)
    def _():
        dtable[...] = jnp.zeros_like(dtable)

    lane = lax.broadcasted_iota(jnp.int32, (TILE, TILE), 1)
    sub = lax.broadcasted_iota(jnp.int32, (TILE, TILE), 0)
    flip = jnp.where(lane + sub == TILE - 1, 1.0, 0.0).astype(LOW)
    keys_t = [jnp.transpose(ref[...].astype(F32)).astype(LOW) for ref in (k0, k1)]
    table_t = jnp.transpose(table[...].astype(F32)).astype(LOW)
    product = do[...].astype(F32) * o[0].astype(F32)
    pieces = []
    gq = []
    for head in range(2):
        inside = in_head(head, q.shape)
        zero = jnp.zeros_like(q)
        query = jnp.where(inside, q[...], zero)
        upstream = jnp.where(inside, do[...], zero)
        ones = jnp.where(in_head(head, (8, TILE)), 1.0, 0.0).astype(F32)
        delta = lax.dot_general(
            ones, product, (((1,), (1,)), ((), ())), precision=lax.Precision.HIGHEST, preferred_element_type=F32
        )[0:1, :]
        level = lse[head : head + 1, :]
        relative = dot_t(query, table[...])
        ends = dot_t(jnp.concatenate([table[0:8, :], table[TILE - 8 :, :]], axis=0), query)
        left_end = ends[0:1, :] - level
        right_end = ends[15:16, :] - level
        far_end = jnp.where(second, left_end, right_end)
        scores[:rows, :] = dot_t(k0[...], query)
        scores[rows:, :] = dot_t(k1[...], query)
        ds_back[:rows, :] = dot_t(v0[...], upstream)
        ds_back[rows:, :] = dot_t(v1[...], upstream)
        for b in range(blocks):
            at = slice(b * TILE, (b + 1) * TILE)
            _, _, band = band_of(relative[at, :])
            turned = [jnp.transpose(item) - level[:, at] for item in band]
            kept = {}
            for t in range(2 * blocks):
                down = slice(t * TILE, (t + 1) * TILE)
                gap = t - b
                if t < blocks:
                    if gap <= -2:
                        term = left_end[:, at]
                    elif gap >= 2:
                        term = right_end[:, at]
                    else:
                        term = turned[gap + 1]
                else:
                    term = far_end[:, at]
                    if b == blocks - 1 and t == blocks:
                        term = jnp.where(second, jnp.broadcast_to(left_end[:, at], (TILE, TILE)), turned[2])
                    if b == 0 and t == 2 * blocks - 1:
                        term = jnp.where(second, turned[0], jnp.broadcast_to(right_end[:, at], (TILE, TILE)))
                value = jnp.exp(scores[down, at] + term)
                prob[down, at] = value.astype(LOW)
                change = (value * (ds_back[down, at] - delta[:, at])).astype(LOW)
                slope[down, at] = change
                if t < blocks and abs(gap) <= 1:
                    kept[gap + 1] = change
                if b == blocks - 1 and t == blocks:
                    kept[2] = jnp.where(second, jnp.zeros_like(change), change)
                if b == 0 and t == 2 * blocks - 1:
                    kept[0] = jnp.where(second, change, jnp.zeros_like(change))
            stretched = jnp.concatenate([dot_t(flip, kept[g]) for g in range(3)] + [jnp.zeros((TILE, TILE), F32)], axis=1)
            back = pltpu.roll(stretched, 3 * TILE + 1 - LEFT, 1, stride=1, stride_axis=0)
            tiles = [back[:, t * TILE : (t + 1) * TILE] for t in range(4)]
            right_sum = tiles[1] + jnp.where(lane < TILE // 2, tiles[2], 0.0)
            left_sum = tiles[3] + jnp.where(lane < TILE // 2, 0.0, tiles[2])
            right_sum = jnp.sum(right_sum, axis=1, keepdims=True)
            left_sum = jnp.sum(left_sum, axis=1, keepdims=True)
            full = tiles[0] + jnp.where(lane == 0, left_sum, 0.0) + jnp.where(lane == TILE - 1, right_sum, 0.0)
            de[:, at] = dot(jnp.transpose(full).astype(LOW), flip)
        here = slice(head * HEAD_DIM, (head + 1) * HEAD_DIM)
        sums = [0.0, 0.0]
        gradient = 0.0
        for side in range(2):
            column = lax.broadcasted_iota(jnp.int32, (16, rows), 1) // TILE
            row = lax.broadcasted_iota(jnp.int32, (16, rows), 0)
            marks = jnp.where(column == row, 1.0, 0.0).astype(LOW)
            mixed = dot(
                jnp.concatenate([keys_t[side][here, :], marks], axis=0),
                slope[side * rows : (side + 1) * rows, :],
            )
            gradient = gradient + mixed[:HEAD_DIM]
            sums[side] = mixed[HEAD_DIM : HEAD_DIM + 8]
        position = lax.broadcasted_iota(jnp.int32, (8, rows), 1) // TILE
        tile_row = lax.broadcasted_iota(jnp.int32, (8, rows), 0)
        gap = tile_row - position
        left_add = jnp.where((gap <= -2) & (tile_row < blocks), sums[0], 0.0)
        right_add = jnp.where((gap >= 2) & (tile_row < blocks), sums[0], 0.0)
        others = jnp.where(tile_row < blocks, sums[1], 0.0)
        left_other = jnp.where((position == 0) & (tile_row == blocks - 1), 0.0, others)
        right_other = jnp.where((position == blocks - 1) & (tile_row == 0), 0.0, others)
        left_add = left_add + jnp.where(second, left_other, 0.0)
        right_add = right_add + jnp.where(second, 0.0, right_other)
        left_add = jnp.sum(left_add, axis=0, keepdims=True)
        right_add = jnp.sum(right_add, axis=0, keepdims=True)
        where = lax.broadcasted_iota(jnp.int32, (TILE, rows), 0)
        de_low = (
            de[...] + jnp.where(where == 0, left_add, 0.0) + jnp.where(where == TILE - 1, right_add, 0.0)
        ).astype(LOW)
        gradient = gradient + dot(table_t[here, :], de_low)
        gq.append(gradient)
        pieces.append(
            (
                dot(slope[:rows, :], q[...]),
                dot(prob[:rows, :], do[...]),
                dot(slope[rows:, :], q[...]),
                dot(prob[rows:, :], do[...]),
                dot(de_low, q[...]),
            )
        )
    turned = jnp.transpose(jnp.concatenate(gq, axis=0))
    kq[...] = (turned * HEAD_DIM**-0.5).astype(LOW)
    chosen = in_head(0, q.shape)
    dk0[...] = jnp.where(chosen, pieces[0][0], pieces[1][0])
    dv0[...] = jnp.where(chosen, pieces[0][1], pieces[1][1])
    dkv1[0] = jnp.where(chosen, pieces[0][2], pieces[1][2]).astype(LOW)
    dkv1[1] = jnp.where(chosen, pieces[0][3], pieces[1][3]).astype(LOW)
    dtable[...] += jnp.where(in_head(0, (TILE, TILE)), pieces[0][4], pieces[1][4])


def attend_back(core, start, q, do, o, kv, kvr, table, lse):
    rows, width = q.shape
    pairs = width // TILE
    half = width // 2
    specs = pair_specs(rows, pairs, start)
    near = pl.BlockSpec((rows, TILE), lambda i, *_: (0, i))
    square = whole((TILE, TILE))
    return launch(
        attend_back_kernel,
        "attend_back",
        (pairs // 2,),
        (q, do, o, kv, kv, kvr, kvr, table, lse),
        [
            specs[0],
            near,
            pl.BlockSpec((1, rows, TILE), lambda i, *_: (start // (pairs // 2), 0, i)),
            *specs,
            square,
            pl.BlockSpec((8, rows), lambda i, *_: (start + i, 0)),
        ],
        [
            shape((rows, half), LOW),
            shape((rows, half), F32),
            shape((rows, half), F32),
            shape((2, rows, half), LOW),
            shape((TILE, TILE), F32),
        ],
        [near, near, near, pl.BlockSpec((2, rows, TILE), lambda i, *_: (0, 0, i)), square],
        scratch=[
            pltpu.VMEM((2 * rows, rows), LOW),
            pltpu.VMEM((2 * rows, rows), LOW),
            pltpu.VMEM((2 * rows, rows), F32),
            pltpu.VMEM((2 * rows, rows), F32),
            pltpu.VMEM((TILE, rows), F32),
        ],
        scalars=(core,),
        flops=10 * rows * rows * width,
    )


def mixer_in_kernel(o0, o1, x, out0, out1, bias, gain, shift, lin0, gate0, lin1, gate1, x2, n, u, sig, edge):
    i = pl.program_id(0)
    count = pl.num_programs(0) // 2

    @pl.when(i == 0)
    def _():
        x2[...] = x[...] + (dot(o0[0], out0[...]) + dot(o1[0], out1[...]) + bias[...])
        norm_into(x2, gain, shift, n)

    def part(lin, gate):
        value = sigmoid(dot(n[...], gate[0]))
        sig[...] = value
        product = dot(n[...], lin[0]) * value
        u[...] = product
        edge[...] = product[product.shape[0] - HALO :]

    pl.when(i < count)(lambda: part(lin0, gate0))
    pl.when(i >= count)(lambda: part(lin1, gate1))


def mixer_in(o, x, out, bias, gain, shift, gated):
    rows, width = x.shape
    half = width // 2
    tile = 256
    count = half // tile
    wide, thin = whole((rows, width)), whole((1, width))
    pick = lambda index, side: pl.BlockSpec(
        (1, width, tile), lambda i: (index, 0, side(i, count))
    )
    column = pl.BlockSpec((rows, tile), lambda i: (0, i))
    return launch(
        mixer_in_kernel,
        "mixer_in",
        (2 * count,),
        (o, o, x, *out, bias, gain, shift, gated[0], gated[0], gated[1], gated[1]),
        [
            pl.BlockSpec((1, rows, half), lambda i: (0, 0, 0)),
            pl.BlockSpec((1, rows, half), lambda i: (1, 0, 0)),
            wide,
            whole((half, width)),
            whole((half, width)),
            thin,
            thin,
            thin,
            pick(0, first_half),
            pick(1, first_half),
            pick(0, second_half),
            pick(1, second_half),
        ],
        [
            shape((rows, width), F32),
            shape((rows, width), LOW),
            shape((rows, width), F32),
            shape((rows, width), F32),
            shape((HALO, width), F32),
        ],
        [
            wide,
            wide,
            column,
            column,
            pl.BlockSpec((HALO, tile), lambda i: (0, (i + count) % (2 * count))),
        ],
        flops=6 * rows * width * width,
    )


def mixer_out_kernel(u, edge, kernel, gain, shift, out0, out1, x2, z, w0, w1, x3, held):
    i = pl.program_id(0)
    rows = u.shape[0]
    taps = kernel.shape[0] - 1
    held[:HALO, :] = edge[...]
    held[HALO:, :] = u[...]
    at = pl.ds(pl.multiple_of(i * TILE, TILE), TILE)
    for start in range(0, rows, CHUNK):
        total = jnp.zeros((CHUNK, TILE), F32)
        for k in range(taps):
            begin = start + k + HALO + 1 - taps
            total = total + kernel[k : k + 1, :] * held[begin : begin + CHUNK, :]
        z[start : start + CHUNK, at] = total

    @pl.when(i == pl.num_programs(0) - 1)
    def _():
        half = out0.shape[0]

        def step(rows_at, carry):
            hat, _ = normed_rows(z[rows_at, :])
            y = hat * gain[...] + shift[...]
            w = (y * sigmoid(y)).astype(LOW)
            w0[rows_at, :] = w[:, :half]
            w1[rows_at, :] = w[:, half:]
            return carry

        row_loop(rows, step)
        x3[...] = x2[...] + (dot(w0[...], out0[...]) + dot(w1[...], out1[...]))


def mixer_out(u, edge, kernel, gain, shift, out, x2):
    rows, width = u.shape
    half = width // 2
    wide, thin = whole((rows, width)), whole((1, width))
    column = lambda height: pl.BlockSpec((height, TILE), lambda i: (0, i))
    return launch(
        mixer_out_kernel,
        "mixer_out",
        (width // TILE,),
        (u, edge, kernel, gain, shift, *out, x2),
        [column(rows), column(HALO), column(kernel.shape[0]), thin, thin]
        + [whole((half, width))] * 2
        + [wide],
        [shape((rows, width), F32)] + [shape((rows, half), LOW)] * 2 + [shape((rows, width), F32)],
        [wide] + [whole((rows, half))] * 2 + [wide],
        scratch=[pltpu.VMEM((rows + HALO, TILE), F32)],
        flops=2 * rows * width * width,
    )


def mixer_mid_kernel(d, out0, out1, z, gain, shift, bz, sums, head):
    half = out0.shape[0]
    rows = d.shape[0]
    bz[:, :half] = dot_t(d[...], out0[...])
    bz[:, half:] = dot_t(d[...], out1[...])

    def step(at, carry):
        hat, inverse = normed_rows(z[at, :])
        y = hat * gain[...] + shift[...]
        gate = sigmoid(y)
        upstream = bz[at, :] * (gate + y * gate * (1.0 - gate))
        scaled = upstream * gain[...]
        first = jnp.mean(scaled, axis=1, keepdims=True)
        second = jnp.mean(scaled * hat, axis=1, keepdims=True)
        bz[at, :] = inverse * (scaled - first - hat * second)
        return carry[0] + fold(upstream * hat), carry[1] + fold(upstream)

    zero = jnp.zeros((8, d.shape[1]), F32)
    first, second = row_loop(rows, step, (zero, zero))
    sums[0:8, :] = first
    sums[8:16, :] = second
    head[:, half:] = bz[:HALO, :half]
    head[:, :half] = bz[:HALO, half:]


def mixer_mid(d, out, z, gain, shift):
    rows, width = d.shape
    half = width // 2
    wide, thin = whole((rows, width)), whole((1, width))
    return launch(
        mixer_mid_kernel,
        "mixer_mid",
        (1,),
        (d, *out, z, gain, shift),
        [wide, whole((half, width)), whole((half, width)), wide, thin, thin],
        [shape((rows, width), F32), shape((16, width), F32), shape((HALO, width), F32)],
        [wide, whole((16, width)), whole((HALO, width))],
        flops=2 * rows * width * width,
    )


def mixer_back_kernel(
    bz, tail, u, edge, kernel, sig, lin0, gate0, lin1, gate1, x2, gain, g, out0, out1,
    own, oth, dkernel, gradient, low, do0, do1, sums, held, later, total, taps_sum, keys,
):
    i = pl.program_id(0)
    count = pl.num_programs(0) // 2
    rows = u.shape[0]
    taps = kernel.shape[0] - 1
    held[:HALO, :] = edge[...]
    held[HALO:, :] = u[...]
    later[:rows, :] = bz[...]
    later[rows:, :] = tail[...]
    taps_sum[...] = jnp.zeros_like(taps_sum)
    for start in range(0, rows, CHUNK):
        here = slice(start, start + CHUNK)
        upstream = later[here, :]
        change = jnp.zeros((CHUNK, TILE), F32)
        for k in range(taps):
            ahead = start + taps - 1 - k
            change = change + kernel[k : k + 1, :] * later[ahead : ahead + CHUNK, :]
            begin = start + k + HALO + 1 - taps
            taps_sum[8 * k : 8 * k + 8, :] += fold(upstream * held[begin : begin + CHUNK, :])
        gate = sig[here, :]
        linear = change * gate
        keys[here, :TILE] = linear.astype(LOW)
        keys[here, TILE:] = (change * held[start + HALO : start + HALO + CHUNK, :] * (1.0 - gate)).astype(LOW)
    dkernel[...] = jnp.sum(taps_sum[...].reshape(kernel.shape[0], 8, TILE), axis=1)

    def part(lin, gate, target, start):
        target[0] = keys[:, :TILE]
        target[1] = keys[:, TILE:]
        product = dot_t(keys[...], jnp.concatenate([lin[0], gate[0]], axis=1))
        if start:
            total[...] = product
        else:
            total[...] += product

    pl.when(i == 0)(lambda: part(lin0, gate0, own, True))
    pl.when((i > 0) & (i < count))(lambda: part(lin0, gate0, own, False))
    pl.when(i >= count)(lambda: part(lin1, gate1, oth, False))

    @pl.when(i == pl.num_programs(0) - 1)
    def _():
        def step(at, carry):
            upstream = total[at, :]
            change, hat = norm_back(upstream, x2[at, :], gain[...])
            value = g[at, :] + change
            gradient[at, :] = value
            rounded = value.astype(LOW)
            low[at, :] = rounded
            return (
                carry[0] + fold(upstream * hat),
                carry[1] + fold(upstream),
                carry[2] + fold(rounded.astype(F32)),
            )

        zero = jnp.zeros((8, x2.shape[1]), F32)
        first, second, third = row_loop(rows, step, (zero, zero, zero))
        sums[0:8, :] = first
        sums[8:16, :] = second
        sums[16:24, :] = third
        do0[...] = dot_t(low[...], out0[...]).astype(LOW)
        do1[...] = dot_t(low[...], out1[...]).astype(LOW)


def mixer_back(bz, tail, u, edge, kernel, sig, gated, x2, gain, g, out):
    rows, width = u.shape
    half = width // 2
    count = half // TILE
    wide, thin = whole((rows, width)), whole((1, width))
    column = lambda height: pl.BlockSpec((height, TILE), lambda i: (0, i))
    pick = lambda index, side: pl.BlockSpec(
        (1, width, TILE), lambda i: (index, 0, side(i, count))
    )
    return launch(
        mixer_back_kernel,
        "mixer_back",
        (2 * count,),
        (bz, tail, u, edge, kernel, sig, gated[0], gated[0], gated[1], gated[1], x2, gain, g, *out),
        [
            column(rows),
            column(HALO),
            column(rows),
            column(HALO),
            column(kernel.shape[0]),
            column(rows),
            pick(0, first_half),
            pick(1, first_half),
            pick(0, second_half),
            pick(1, second_half),
            wide,
            thin,
            wide,
            whole((half, width)),
            whole((half, width)),
        ],
        [
            shape((2, rows, half), LOW),
            shape((2, rows, half), LOW),
            shape(kernel.shape, F32),
            shape((rows, width), F32),
            shape((rows, width), LOW),
            shape((rows, half), LOW),
            shape((rows, half), LOW),
            shape((24, width), F32),
        ],
        [
            pl.BlockSpec((2, rows, TILE), lambda i: (0, 0, first_half(i, count))),
            pl.BlockSpec((2, rows, TILE), lambda i: (0, 0, second_half(i, count))),
            column(kernel.shape[0]),
            wide,
            wide,
            whole((rows, half)),
            whole((rows, half)),
            whole((24, width)),
        ],
        scratch=[
            pltpu.VMEM((rows + HALO, TILE), F32),
            pltpu.VMEM((rows + HALO, TILE), F32),
            pltpu.VMEM((rows, width), F32),
            pltpu.VMEM((8 * kernel.shape[0], TILE), F32),
            pltpu.VMEM((rows, 2 * TILE), LOW),
        ],
        flops=6 * rows * width * width,
    )


def project_back_kernel(
    kq0, dk0, dv0, far0, kq1, dk1, dv1, far1, qw0, kw0, vw0, qw1, kw1, vw1, x, gain, g,
    own, oth, gradient, low, sums, total,
):
    i = pl.program_id(0)
    count = pl.num_programs(0) // 2
    rows = x.shape[0]
    step = kq0.shape[1]
    at = pl.ds(pl.multiple_of(i * step, TILE), step)

    def part(kq, dk, dv, far, qw, kw, vw, target, start):
        kk = (dk[...] + far[0].astype(F32)).astype(LOW)
        kv = (dv[...] + far[1].astype(F32)).astype(LOW)
        target[0] = kk
        target[1] = kv
        product = dot_t(kq[...], qw[...]) + dot_t(kk, kw[...]) + dot_t(kv, vw[...])
        if start:
            total[...] = product
        else:
            total[...] += product
        ones = jnp.ones((8, rows), LOW)
        sums[16:24, at] = dot(ones, kq[...]) * 0.125
        sums[24:32, at] = dot(ones, kv) * 0.125

    first = (kq0, dk0, dv0, far0, qw0, kw0, vw0, own)
    pl.when(i == 0)(lambda: part(*first, True))
    pl.when((i > 0) & (i < count))(lambda: part(*first, False))
    pl.when(i >= count)(lambda: part(kq1, dk1, dv1, far1, qw1, kw1, vw1, oth, False))

    @pl.when(i == pl.num_programs(0) - 1)
    def _():
        def step(rows_at, carry):
            upstream = total[rows_at, :]
            change, hat = norm_back(upstream, x[rows_at, :], gain[...])
            value = g[rows_at, :] + change
            gradient[rows_at, :] = value
            low[rows_at, :] = (0.5 * value).astype(LOW)
            return carry[0] + fold(upstream * hat), carry[1] + fold(upstream)

        zero = jnp.zeros((8, x.shape[1]), F32)
        first, second = row_loop(rows, step, (zero, zero))
        sums[0:8, :] = first
        sums[8:16, :] = second


def project_back(own, oth, qw, kw, vw, x, gain, g):
    rows, width = x.shape
    half = width // 2
    tile = 256
    count = half // tile
    wide, thin = whole((rows, width)), whole((1, width))

    def flat(side):
        return pl.BlockSpec((rows, tile), lambda i: (0, side(i, count)))

    def stacked(side):
        return pl.BlockSpec((2, rows, tile), lambda i: (0, 0, side(i, count)))

    weight = lambda side: pl.BlockSpec((width, tile), lambda i: (0, side(i, count)))
    return launch(
        project_back_kernel,
        "project_back",
        (2 * count,),
        (*own, *oth, qw[0], kw[0], vw[0], qw[1], kw[1], vw[1], x, gain, g),
        [flat(first_half)] * 3
        + [stacked(first_half)]
        + [flat(second_half)] * 3
        + [stacked(second_half)]
        + [weight(first_half)] * 3
        + [weight(second_half)] * 3
        + [wide, thin, wide],
        [
            shape((2, rows, half), LOW),
            shape((2, rows, half), LOW),
            shape((rows, width), F32),
            shape((rows, width), LOW),
            shape((32, width), F32),
        ],
        [stacked(first_half), stacked(second_half), wide, wide, whole((32, width))],
        scratch=[pltpu.VMEM((rows, width), F32)],
        flops=6 * rows * width * width,
    )


def bit_order(devices, color):
    first = ((0, 1, 2), (1, 0, 2), (0, 1, 2), (1, 2, 0), (2, 0, 1))[color]
    return [*first, *range(3, devices.bit_length() - 1)]


def weight_kernel(devices, plan, sides, pairs, me, *refs):
    used = sorted({color for _, _, color in plan})
    places = sorted({(side, color) for side, _, color in plan})
    lefts, refs = refs[: 2 * sides], refs[2 * sides :]
    inputs, refs = refs[: 2 * pairs], refs[2 * pairs :]
    outs, turned = refs[: 2 * len(used)], refs[2 * len(used) :]
    rows, width = lefts[0].shape
    block = width // devices
    half = width // 2
    i = pl.program_id(0)

    def arrange(side):
        colors = [color for item, color in places if item == side]
        for part, source in enumerate(lefts[2 * side : 2 * side + 2]):
            for lane in range(0, width, TILE):
                piece = jnp.transpose(source[:, lane : lane + TILE].astype(F32)).astype(LOW)
                for inner in range(0, TILE, block):
                    relative = ((lane + inner) // block) ^ me[0]
                    for color in colors:
                        place = 0
                        for level, bit in enumerate(bit_order(devices, color)):
                            flag = 1 - ((relative >> bit) & 1)
                            place = place + flag * (devices >> (level + 1))
                        start = pl.multiple_of(place * block, block)
                        turned[places.index((side, color))][
                            pl.ds(start, block), part * rows : (part + 1) * rows
                        ] = piece[inner : inner + block, :]

    for step, (side, source, color) in enumerate(plan):
        fresh = side not in [item[0] for item in plan[:step]]

        def work(side=side, source=source, color=color, fresh=fresh):
            if fresh:
                arrange(side)
            q0, q1 = (ref if len(ref.shape) == 2 else ref.at[0] for ref in inputs[2 * source : 2 * source + 2])
            left = turned[places.index((side, color))]
            slot = used.index(color)
            product = dot(left[:, :rows], q0[...]) + dot(left[:, rows:], q1[...])
            outs[2 * slot][...] = product[:half].astype(LOW)
            outs[2 * slot + 1][...] = product[half:].astype(LOW)

        pl.when(i == step)(work)


def weight_gradient(devices, me, lefts, jobs, tile):
    rows, width = lefts[0][0].shape
    specs, operands, plan = [whole((rows, width))] * (2 * len(lefts)), [item for pair in lefts for item in pair], []
    for source, (side, pair, colors) in enumerate(jobs):
        first, last = len(plan), len(colors) - 1
        if pair[0].ndim == 2:
            spec = pl.BlockSpec((rows, tile), lambda i, *_, f=first, t=last: (0, jnp.clip(i - f, 0, t)))
        else:
            per = pair[0].shape[2] // tile

            def pick(i, *_, f=first, t=last, per=per):
                place = jnp.clip(i - f, 0, t)
                return place // per, 0, place % per

            spec = pl.BlockSpec((1, rows, tile), pick)
        specs += [spec, spec]
        operands += list(pair)
        plan += [(side, source, color) for color in colors]
    used = sorted({color for _, _, color in plan})
    outs, out_specs = [], []
    for color in used:
        steps = [step for step, item in enumerate(plan) if item[2] == color]

        def column(i, *_, steps=steps):
            place = 0
            for step in steps[1:]:
                place = place + jnp.where(i >= step, 1, 0)
            return 0, place

        outs += [shape((width // 2, tile * len(steps)), LOW)] * 2
        out_specs += [pl.BlockSpec((width // 2, tile), column)] * 2
    places = {(side, color) for side, _, color in plan}
    return launch(
        functools.partial(weight_kernel, devices, plan, len(lefts), len(jobs)),
        "weight_gradient",
        (len(plan),),
        operands,
        specs,
        outs,
        out_specs,
        scratch=[pltpu.VMEM((width, 2 * rows), LOW)] * len(places),
        scalars=(me,),
        flops=4 * rows * width * tile * len(plan),
    )


def gather_kernel(early, late, query_bias, value_bias, gain, shift, kernel, out):
    width = query_bias.shape[1]
    out[0:1, :] = early[...]
    out[1:2, :] = late[...]
    for slot, item in enumerate((query_bias, value_bias, gain, shift)):
        out[2 + slot : 3 + slot, :width] = item[...]
    out[8 : 8 + kernel.shape[0], :width] = kernel[...]


def gather(early, late, items, kernel):
    operands = (early, late, *items, kernel)
    rows = 8 + (kernel.shape[0] + 7) // 8 * 8
    return launch(
        gather_kernel,
        "gather",
        (1,),
        operands,
        [whole(item.shape) for item in operands],
        [shape((rows, early.shape[1]), F32)],
        [whole((rows, early.shape[1]))],
    )[0]


def swap(values):
    return lax.ppermute(values, "tensor", [(0, 1), (1, 0)])


def cross(values, devices, mask):
    return lax.ppermute(values, "dp", [(i, i ^ mask) for i in range(devices)])


def whole_slice(devices, block):
    return devices & (devices - 1) or devices < 8 or block % 16 or TILE % block


class Reduction:
    def __init__(self, devices, me, lefts, jobs, tile=512):
        self.devices = devices
        self.tile = tile
        self.colors = sorted({color for _, _, colors in jobs for color in colors})
        self.order = {color: [] for color in self.colors}
        for job, (_, pair, colors) in enumerate(jobs):
            for place, color in enumerate(colors):
                self.order[color].append((job, place))
        self.level = 0
        self.rows = lefts[0][0].shape[1]
        self.state = []
        self.result = None
        if whole_slice(devices, lefts[0][0].shape[1] // devices):
            pieces = []
            for side, pair, colors in jobs:
                both = jnp.concatenate([item if item.ndim == 2 else item[: -(-tile * len(colors) // item.shape[2])] for item in pair], axis=-2)
                if both.ndim == 3:
                    both = jnp.concatenate(list(both), axis=1)[:, : tile * len(colors)]
                left = jnp.concatenate(lefts[side], axis=0)
                pieces.append(dot(left, both, ((0,), (0,))).astype(LOW))
            total = lax.psum_scatter(jnp.concatenate(pieces, axis=1), "dp", scatter_dimension=0, tiled=True)
            cuts = [0]
            for piece in pieces:
                cuts.append(cuts[-1] + piece.shape[1])
            self.result = [total[:, a:b].astype(F32) for a, b in zip(cuts, cuts[1:])]
            return
        parts = weight_gradient(devices, me, lefts, jobs, tile)
        self.state = list(parts)

    def send(self):
        if self.result is not None:
            return
        for slot in range(len(self.state) // 2):
            bit = bit_order(self.devices, self.colors[slot])[self.level]
            self.state[2 * slot] = cross(self.state[2 * slot], self.devices, 1 << bit)

    def add(self):
        if self.result is not None:
            return
        self.level += 1
        arrived, kept = self.state[::2], self.state[1::2]
        half = kept[0].shape[0] // 2
        if half * 2 * self.devices == self.rows:
            self.state = [arrived[0].astype(F32) + kept[0].astype(F32)]
            return
        away = [one[:half] + two[:half] for one, two in zip(arrived, kept)]
        stay = [one[half:] + two[half:] for one, two in zip(arrived, kept)]
        bits = {bit_order(self.devices, color)[self.level] for color in self.colors}
        if len(bits) == 1 and len(away) > 1:
            away, stay = [jnp.concatenate(away, axis=1)], [jnp.concatenate(stay, axis=1)]
        self.state = [item for pair in zip(away, stay) for item in pair]

    def parts(self):
        if self.result is not None:
            return self.result
        tile = self.tile
        found = {}
        keys = [key for color in self.colors for key in self.order[color]]
        for column, key in enumerate(keys):
            found[key] = self.state[0][:, column * tile : (column + 1) * tile]
        jobs = sorted({job for job, _ in found})
        return [
            jnp.concatenate([found[key] for key in sorted(found) if key[0] == job], axis=1) for job in jobs
        ]


def hold(main, *reductions):
    flat = list(main)
    for item in reductions:
        flat += item.state
    flat = lax.optimization_barrier(tuple(flat))
    place = len(main)
    for item in reductions:
        count = len(item.state)
        item.state = list(flat[place : place + count])
        place += count
    return flat[: len(main)]


def pack_kernel(late, final, mixer, attended, depth, early, dkernel, dtable0, dtable1, t10, t11, t40, t41, own, oth, table):
    width = late.shape[1]
    half = width // 2
    own[...] = jnp.zeros_like(own)
    oth[...] = jnp.zeros_like(oth)
    rolled = dtable0[...] + dtable1[...]
    table[0:REL, :] = rolled[0:REL]
    table[REL - 1 : REL, :] = jnp.sum(rolled[REL - 1 :], axis=0, keepdims=True)
    table[REL:, :] = jnp.zeros((table.shape[0] - REL, TILE), F32)

    def folded(source, group):
        return jnp.sum(source[8 * group : 8 * group + 8, :], axis=0, keepdims=True)

    shared = [folded(late, g) for g in range(3)] + [folded(final, g) for g in range(2)]
    shared += [folded(mixer, g) for g in range(3)] + [folded(attended, g) for g in range(2)]
    shared += [folded(early, g) for g in range(3)]
    mixed = [folded(attended, g) for g in (2, 3)] + [folded(depth, g) for g in range(2)]
    for target, start, tallies in ((own, 0, (t10, t40)), (oth, half, (t11, t41))):
        for place, item in enumerate(shared):
            target[place : place + 1, :] = item
        for g in range(8):
            target[SHARED - 11 : SHARED - 1, g * TILE : (g + 1) * TILE] = table[10 * g : 10 * g + 10, :]
        for place, item in enumerate(mixed):
            target[SHARED + place : SHARED + place + 1, :half] = item[:, start : start + half]
        target[SHARED + 4 : SHARED + 18, :half] = dkernel[0:14, start : start + half]
        target[SHARED : SHARED + 17, half:] = dkernel[14:31, start : start + half]
        place = SHARED + 18
        for item in tallies:
            for begin in range(0, item.shape[1], width):
                target[place : place + 1, :] = item[0:1, begin : begin + width]
                place += 1


def pack(operands):
    width = operands[0].shape[1]
    rows = SHARED + 24
    return launch(
        pack_kernel,
        "pack",
        (1,),
        operands,
        [whole(item.shape) for item in operands],
        [shape((rows, width), F32)] * 2,
        [whole((rows, width))] * 2,
        scratch=[pltpu.VMEM((80, TILE), F32)],
    )


def shards(
    devices,
    inputs,
    cotangent,
    slot_flags,
    early_norm_gain,
    early_norm_shift,
    early_up,
    early_up_bias,
    early_down,
    early_down_bias,
    attend_norm_gain,
    attend_norm_shift,
    query_weight,
    query_bias,
    key_weight,
    value_weight,
    value_bias,
    distance_table,
    attend_weight,
    attend_bias,
    mixer_norm_gain,
    mixer_norm_shift,
    gated_weight,
    depth_kernel,
    depth_norm_gain,
    depth_norm_shift,
    mixer_weight,
    late_norm_gain,
    late_norm_shift,
    late_up,
    late_up_bias,
    late_down,
    late_down_bias,
    final_gain,
    final_shift,
):
    row = lambda vector: vector[None, :]
    both = lambda weight: (weight, swap(weight))
    side = lax.axis_index("tensor").astype(jnp.int32)
    core = side[None]
    me = lax.axis_index("dp").astype(jnp.int32)[None]
    half = depth_kernel.shape[1]
    hidden = early_up.shape[1]
    taps = depth_kernel.shape[0]

    vectors = (query_bias, value_bias, depth_norm_gain, depth_norm_shift)
    small = gather(row(early_up_bias), row(late_up_bias), [row(item) for item in vectors], depth_kernel)
    other = swap(small)
    early_bias = (row(early_up_bias), other[0:1])
    late_bias = (row(late_up_bias), other[1:2])
    query_bias_all, value_bias_all, depth_gain_all, depth_shift_all = [
        jnp.concatenate([row(item), other[2 + slot : 3 + slot, :half]], axis=1)
        for slot, item in enumerate(vectors)
    ]
    kernel_all = jnp.concatenate([small[8 : 9 + taps, :half], other[8 : 9 + taps, :half]], axis=1)
    early_up_all, early_down_all = both(early_up), both(early_down)
    key_all, value_all, query_all = both(key_weight), both(value_weight), both(query_weight)
    table = distance_table.astype(LOW)
    table = jnp.concatenate([table, jnp.broadcast_to(table[REL - 1 :], (TILE - REL, HEAD_DIM))], axis=0)
    table = jnp.concatenate([table, table], axis=1)

    n1, s10, a10, x1 = feed_half(
        True, inputs, (row(early_norm_gain), row(early_norm_shift)), early_up_all[0], early_bias[0], early_down_all[0]
    )
    s11, a11, x1 = feed_half(
        False, inputs, (n1, x1, row(early_down_bias)), early_up_all[1], early_bias[1], early_down_all[1]
    )
    n2, kv = project(x1, row(attend_norm_gain), row(attend_norm_shift), key_all, value_all, value_bias_all)
    kv, query_other = hold((kv, query_all[1]))
    query_all = (query_weight, query_other)
    kvr = swap(kv)
    q = query(n2, query_all, query_bias_all)
    attend_all, gated_all = both(attend_weight), both(gated_weight)
    o, lse = attend(core, q, kv, kvr, table)
    o, late_up, late_down, mixer_weight, attend_other, gated_other = hold(
        (o, late_up, late_down, mixer_weight, attend_all[1], gated_all[1])
    )
    attend_all, gated_all = (attend_weight, attend_other), (gated_weight, gated_other)
    mixer_all = both(mixer_weight)
    late_up_all, late_down_all = both(late_up), both(late_down)
    n1p, a1p, n2p = swap(n1), swap(a11), swap(n2)
    x2, n3, u, sig, edge = mixer_in(
        o, x1, attend_all, row(attend_bias), row(mixer_norm_gain), row(mixer_norm_shift), gated_all
    )
    edge = lax.ppermute(edge, "tensor", [(0, 1)])
    op, n3p = swap(o[1:]), swap(n3)
    z, w0, w1, x3 = mixer_out(u, edge, kernel_all, depth_gain_all, depth_shift_all, mixer_all, x2)
    wp = swap(w1)
    x3, n1p, a1p, n2p = hold((x3, n1p, a1p, n2p))
    n4, s40, s41, a40, a41, x4 = feed_forward(
        x3, row(late_norm_gain), row(late_norm_shift), late_up_all, late_bias, late_down_all, row(late_down_bias)
    )
    n4p, a4p = swap(n4), swap(a41)
    x4, op, n3p, wp = hold((x4, op, n3p, wp))
    output, g4, d4, final_sums = final_norm(slot_flags, x4, cotangent, row(final_gain), row(final_shift))
    d4p = swap(d4)

    reduction = functools.partial(Reduction, devices, me)
    k40, k41, t40, t41, g3, d3, late_sums = feed_back(
        1.0, g4, d4, x3, row(late_norm_gain), late_up_all, late_down_all, (s40, s41)
    )
    k4p, d3p = swap(k41), swap(d3)
    bz, depth_sums, head = mixer_mid(d3, mixer_all, z, depth_gain_all, depth_shift_all)
    tail = lax.ppermute(head, "tensor", [(1, 0)])
    bz, d4p, n4p, a4p, k4p, d3p = hold((bz, d4p, n4p, a4p, k4p, d3p))
    one = reduction(
        [(d4, d4p), (n4, n4p)], [(0, (a40, a4p), (2, 2, 2, 3)), (1, (k40, k4p), (3, 3, 4, 4))]
    )
    bz, tail = hold((bz, tail), one)
    one.send()
    ka0, ka1, dkernel, g2, d2, do0, do1, mixer_sums = mixer_back(
        bz, tail, u, edge, kernel_all, sig, gated_all, x2, row(mixer_norm_gain), g3, attend_all
    )
    kap, d2p = swap(ka1), swap(d2)
    kq0, dk0, dv0, dkv0, dtable0 = attend_back(core, 0, q, do0, o, kv, kvr, table, lse)
    kq0, kap, d2p = hold((kq0, kap, d2p), one)
    far1 = swap(dkv0)
    three = reduction(
        [(d3, d3p), (n3, n3p), (d2, d2p)],
        [(0, (w0, wp), (0,)), (1, (ka0, kap), (0, 1)), (2, (o, op), (1,))],
    )
    one.add()
    do1, kq0, far1 = hold((do1, kq0, far1), one, three)
    one.send()
    three.send()
    kq1, dk1, dv1, dkv1, dtable1 = attend_back(core, q.shape[1] // TILE // 2, q, do1, o, kv, kvr, table, lse)
    kq1, dkv1 = hold((kq1, dkv1), one)
    far0, kqp = swap(dkv1), swap(kq1)
    one.add()
    dk0, far0 = hold((dk0, far0), one)
    one.send()
    kk0, kk1, g1, d1, attend_sums = project_back(
        (kq0, dk0, dv0, far0), (kq1, dk1, dv1, far1), query_all, key_all, value_all, x1, row(attend_norm_gain), g2
    )
    d1p, kkp = swap(d1), swap(kk1)
    (g1,) = hold((g1,), one, three)
    one.add()
    three.add()
    d1p, kkp = hold((d1p, kkp), one, three)
    one.send()
    three.send()
    four = reduction(
        [(d1, d1p), (n2, n2p)],
        [
            (0, (a10, a1p), (2, 2, 2, 3, 3, 3, 4, 4)),
            (1, (kq0, kqp), (2, 2)),
            (1, (kk0, kkp), (3, 3, 4, 4)),
        ],
        256,
    )
    (d1,) = hold((d1,), four, one, three)
    four.send()
    one.add()
    three.add()
    three.send()
    k10, k11, t10, t11 = feed_key(d1, early_down_all, (s10, s11))
    k1p = swap(k11)
    gradient, early_sums = feed_end(g1, d1, inputs, row(early_norm_gain), early_up_all, (k10, k11))
    (early_sums,) = hold((early_sums,), four, three)
    four.add()
    three.add()
    n1, k1p = hold((n1, k1p), four, three)
    four.send()
    three.send()
    five = reduction([(n1, n1p)], [(0, (k10, k1p), (2, 2, 2, 3, 3, 3, 4, 4))], 256)
    three.add()
    (early_sums,) = hold((early_sums,), five, three)
    five.send()
    small_own, small_oth = pack(
        (
            late_sums, final_sums, mixer_sums, attend_sums, depth_sums, early_sums, dkernel,
            dtable0, dtable1, t10, t11, t40, t41,
        )
    )
    first = small_own
    masks = [1 << bit for bit in (3, 0, 1, 2, *range(4, devices.bit_length() - 1))]
    if devices & (devices - 1) or devices < 16:
        masks = []
    moved = swap(small_oth)
    for step in range(4):
        first = first + moved
        if step == 2:
            late_down_sum, late_up_sum = one.parts()
            mixer_sum, gated_sum, attend_sum = three.parts()
            gated_sum = jnp.stack([gated_sum[:, :half], gated_sum[:, half:]])
            done = (late_down_sum.T, late_up_sum, mixer_sum.T, gated_sum, attend_sum.T)
            first, *done = hold((first, *done))
            late_down_sum, late_up_sum, mixer_sum, gated_sum, attend_sum = done
        if step == 3:
            early_down_sum, query_sum, project_sum = four.parts()
            done = (early_down_sum.T, query_sum, project_sum[:, :half], project_sum[:, half:])
            first, *done = hold((first, *done))
            early_down_sum, query_sum, key_sum, value_sum = done
        moved = cross(first, devices, masks[step]) if masks else jnp.zeros_like(first)
        if step < 3:
            four.add()
        if step < 2:
            four.send()
        five.add()
        (first,) = hold((first,), four, five)
        if step < 3:
            five.send()
    first = first + moved
    for mask in masks[4:]:
        first = first + cross(first, devices, mask)
    if not masks:
        first = lax.psum(first, "dp")
    (early_up_sum,) = five.parts()

    table_out = jnp.concatenate(
        [first[SHARED - 11 : SHARED - 1, g * TILE : (g + 1) * TILE] for g in range(8)], axis=0
    )[:REL]
    table_out = table_out[:, :HEAD_DIM] + table_out[:, HEAD_DIM:]
    left, right = first[SHARED : SHARED + 18, :half], first[SHARED : SHARED + 17, half:]
    pile_sum = jnp.concatenate([left, right], axis=0)
    early_rows = first[10:13]
    count = hidden // (2 * half)
    early_up_bias_sum = first[SHARED + 18 : SHARED + 18 + count].reshape(-1)
    late_up_bias_sum = first[SHARED + 18 + count : SHARED + 18 + 2 * count].reshape(-1)
    return (
        output,
        gradient,
        early_rows[0],
        early_rows[1],
        early_up_sum,
        early_up_bias_sum,
        early_down_sum,
        early_rows[2],
        first[8],
        first[9],
        query_sum,
        pile_sum[0],
        key_sum,
        value_sum,
        pile_sum[1],
        table_out,
        attend_sum,
        first[7],
        first[5],
        first[6],
        gated_sum,
        pile_sum[4:],
        pile_sum[2],
        pile_sum[3],
        mixer_sum,
        first[0],
        first[1],
        late_up_sum,
        late_up_bias_sum,
        late_down_sum,
        first[2],
        first[3],
        first[4],
    )


def solution(mesh):
    placed = (
        P(("dp", "tensor"), None),
        P(("dp", "tensor"), None),
        P("dp"),
        P(),
        P(),
        P(None, "tensor"),
        P("tensor"),
        P("tensor", None),
        P(),
        P(),
        P(),
        P(None, "tensor"),
        P("tensor"),
        P(None, "tensor"),
        P(None, "tensor"),
        P("tensor"),
        P(),
        P("tensor", None),
        P(),
        P(),
        P(),
        P(None, None, "tensor"),
        P(None, "tensor"),
        P("tensor"),
        P("tensor"),
        P("tensor", None),
        P(),
        P(),
        P(None, "tensor"),
        P("tensor"),
        P("tensor", None),
        P(),
        P(),
        P(),
    )
    return jax.shard_map(
        functools.partial(shards, mesh.shape["dp"]),
        mesh=mesh,
        in_specs=placed,
        out_specs=(
            P(("dp", "tensor"), None),
            P(("dp", "tensor"), None),
            P(),
            P(),
            P("dp", "tensor"),
            P("tensor"),
            P("tensor", "dp"),
            P(),
            P(),
            P(),
            P("dp", "tensor"),
            P("tensor"),
            P("dp", "tensor"),
            P("dp", "tensor"),
            P("tensor"),
            P(),
            P("tensor", "dp"),
            P(),
            P(),
            P(),
            P(None, "dp", "tensor"),
            P(None, "tensor"),
            P("tensor"),
            P("tensor"),
            P("tensor", "dp"),
            P(),
            P(),
            P("dp", "tensor"),
            P("tensor"),
            P("tensor", "dp"),
            P(),
            P(),
            P(),
        ),
        check_vma=False,
    )
```
